32 devices in a mesh: member: 2 (over core), atm: 4 (over z), ocn: 4 (over y, x).
Axes of the slice: x: 2, y: 2, z: 4, core: 2. Of those that a mesh axis runs over, the one named last changes fastest.
Arguments:
- atmos_state: float32 [4, 137, 65536], P(None, None, ('member', 'atm', 'ocn')), parts along dimension 2, may hold values from -6 to 6
- inverses: float32 [4, 4, 137, 137], P('atm'), may hold values from -1 to 2
- flux_weight: float32 [4, 137, 128], replicated, may hold values from -0.25 to 0.25
- surface_weight: float32 [4, 137, 128], replicated, may hold values from -0.5 to 0.5
- area_table: float32 [64], replicated, may hold values from 0.25 to 1
- xc_column: int32 [65536], P(('atm', 'ocn')), may hold values from 0 to 2047, as said below
- xc_dest: int32 [65536, 1], P(('atm', 'ocn')), may hold values from 0 to 15, as said below
- xc_cell: int32 [65536], P(('atm', 'ocn')), may hold values from 0 to 4095, as said below
- xc_class: int32 [65536], P(('atm', 'ocn')), may hold values from 0 to 63
- tracer: float32 [75, 128, 1024], P(None, 'atm', ('member', 'ocn')), parts along dimension 2, may hold values from -6 to 6
- land_sea: int32 [128, 512], P('atm', 'ocn'), may hold values 0 or 1
- forcing_weight: float32 [75, 128], replicated, may hold values from -0.25 to 0.25
- surface_map: float32 [75, 128], replicated, may hold values from -0.75 to 0.75
- diffusivity: float32 [75], replicated, may hold values from 0.04 to 0.24
Outputs:
- final_state: float32 [4, 137, 65536], P(None, None, ('member', 'atm', 'ocn')), parts along dimension 2
- tracer_out: float32 [75, 128, 1024], P(None, 'atm', ('member', 'ocn')), parts along dimension 2
The draws below stay inside these ranges and needn't reach their ends.
There are 2 independent parts, one for each index of `member`. The reference program is written for one: setup_inputs(seed, part) draws one part's arguments, and reference() takes and returns one part's arrays. A program takes and returns all parts, laid end to end along the dimension named above; an argument that names none is the same for every part. Nothing has to cross between parts.
Inputs may be any that keep to these rules, and one draw needn't show every extreme that they name: `xc_column`: each column of a device is named by exactly two of that device's exchange cells. `xc_dest`: the exchange cells of the device at index r along atm and index q along ocn name only ocean tiles r * 4 to r * 4 + 3; the tile r * 4 + q gets exactly 3072 of them and every other tile at most 3072; all devices of one index along atm send equally many cells to the tiles at the same offset along ocn, counted modulo 4. `xc_cell`: every ocean cell of the grid is named by exactly one exchange cell, together with xc_dest.
All inputs are finite; a program needn't handle non-finite values. No bound on the sum of `land_sea` on one device may be relied on, other than what follows from the above.
Results may differ from the reference program's by a relative error of at most 0.0025.
Values may be sent and summed in bfloat16 or wider, within the bound.
No kernel may reach another device: no remote copies, remote signals or barrier semaphores. Data moves between devices by JAX's collectives and lax.ppermute only.
A program may use at most 128 MiB of HBM per device.

```python
import math
import jax
import jax.numpy as jnp
from jax import lax

NVAR = 4
K = 137
L = 75
FLUX = 128
NAREA = 64
OSTEPS = 4
COL_DEV = 2048
OX = 128
OY = 32
XC_DEV = 4096
CAP = 3072
XCELLS = 65536
NCOLS = 32768
NY = 128
NX = 512
N_ATM = 4
N_OCN = 4


def draw_inverses(key, part):
    eye_matrix = jnp.eye(K, dtype=jnp.float32)
    base = jnp.clip(jax.random.normal(key, (N_ATM, NVAR, K, K), jnp.float32), -4.0, 4.0)
    return eye_matrix + 0.3 * K ** (-0.5) * base


def shuffles(key, fold_value):
    keys = jax.random.split(jax.random.fold_in(key, fold_value), N_ATM * N_OCN)

    def one_order(single):
        return jax.random.permutation(single, XC_DEV)
    return jax.vmap(one_order)(keys).reshape(N_ATM, N_OCN, XC_DEV).astype(jnp.int32)


def exchange_layout(key):
    weights = jax.random.randint(jax.random.fold_in(key, 11), (N_ATM, N_OCN), 1, 3, dtype=jnp.int32)
    weights = weights * (jnp.arange(N_OCN, dtype=jnp.int32) > 0).astype(jnp.int32)[None, :]
    total_weight = jnp.sum(weights, axis=1, keepdims=True)
    bounds = CAP + (XC_DEV - CAP) * jnp.cumsum(weights, axis=1) // total_weight
    position = jnp.arange(XC_DEV, dtype=jnp.int32)
    offset = jnp.sum((position[None, None, :] >= bounds[:, :, None]).astype(jnp.int32), axis=1)
    tile_order = shuffles(key, 21)
    slot_order = shuffles(key, 31)
    column_order = shuffles(key, 41)
    row_index = jnp.arange(N_ATM, dtype=jnp.int32)[:, None, None]
    own_index = jnp.arange(N_OCN, dtype=jnp.int32)[None, :, None]
    step_off = offset[row_index, slot_order]
    dest_col = (own_index + step_off) % N_OCN
    cell = tile_order[row_index, dest_col, slot_order]
    dest = row_index * N_OCN + dest_col
    column = column_order // 2
    return (column.reshape(-1).astype(jnp.int32), dest.reshape(-1, 1).astype(jnp.int32), cell.reshape(-1).astype(jnp.int32))


def draw_xc_column(key, part):
    return exchange_layout(key)[0]


def draw_xc_dest(key, part):
    return exchange_layout(key)[1]


def draw_xc_cell(key, part):
    return exchange_layout(key)[2]


def set_ends(drawn, key, smallest, largest):
    spot = [jax.random.randint(jax.random.fold_in(key, axis), (), 0, length) for axis, length in enumerate(drawn.shape)]
    widest = drawn.shape.index(max(drawn.shape))
    next_to = spot[:widest] + [(spot[widest] + 1) % drawn.shape[widest]] + spot[widest + 1:]
    return drawn.at[tuple(spot)].set(smallest).at[tuple(next_to)].set(largest)


def block_scale(rng, dims, cuts, low, largest):
    def one(dim, parts):
        heights = jax.random.uniform(jax.random.fold_in(jax.random.fold_in(rng, 6), dim), (parts,), jnp.float32, low / len(cuts), largest / len(cuts))
        return jnp.repeat(jnp.exp(heights), dims[dim] // parts).reshape((-1,) + (1,) * (len(dims) - dim - 1))

    level = one(*cuts[0])
    for cut in cuts[1:]:
        level = level * one(*cut)
    return level


def scatter_about(stream_key, shape, deviation, bound, shards=(), kind=jnp.bfloat16):
    values = jax.random.normal(stream_key, shape, jnp.float32) * deviation
    if len(shards) > 0:
        values = block_scale(stream_key, shape, shards, -0.22, 0.18) * values
    return jnp.clip(values, min=-bound, max=bound).astype(kind)


def setup_inputs(seed: int = 0, part: int = 0) -> dict:
    splits = jax.random.split(jax.random.key(seed), 15)
    part_splits = jax.random.split(jax.random.fold_in(splits[14], part), 15)
    return {
        "atmos_state": scatter_about(part_splits[0], (NVAR, K, NCOLS), 1.0, 6.0, ((2, 16),), jnp.float32),
        "inverses": draw_inverses(jax.random.fold_in(splits[14], 71), part),
        "flux_weight": scatter_about(splits[2], (NVAR, K, FLUX), (NVAR * K) ** -0.5, 0.25, (), jnp.float32),
        "surface_weight": scatter_about(splits[3], (NVAR, K, FLUX), FLUX ** -0.5, 0.5, (), jnp.float32),
        "area_table": jnp.clip(jnp.exp(jax.random.uniform(splits[4], (NAREA,), jnp.float32, math.log(0.25), math.log(1.0))), 0.25, 1.0),
        "xc_column": draw_xc_column(jax.random.fold_in(splits[14], 71), part),
        "xc_dest": draw_xc_dest(jax.random.fold_in(splits[14], 71), part),
        "xc_cell": draw_xc_cell(jax.random.fold_in(splits[14], 71), part),
        "xc_class": set_ends(jax.random.randint(splits[8], (XCELLS,), 0, NAREA), jax.random.fold_in(splits[8], 1), 0, NAREA - 1).astype(jnp.int32),
        "tracer": scatter_about(part_splits[9], (L, NY, NX), 1.0, 6.0, ((1, 4), (2, 4)), jnp.float32),
        "land_sea": set_ends((jax.random.randint(splits[10], (NY, NX), 0, 4) < 3).astype(jnp.int32), jax.random.fold_in(splits[10], 1), 0, 1),
        "forcing_weight": scatter_about(splits[11], (L, FLUX), (4 * FLUX) ** -0.5, 0.25, (), jnp.float32),
        "surface_map": scatter_about(splits[12], (L, FLUX), L ** -0.5, 0.75, (), jnp.float32),
        "diffusivity": jnp.clip(jnp.exp(jax.random.uniform(splits[13], (L,), jnp.float32, math.log(0.04), math.log(0.24))), 0.04, 0.24),
    }


highest = lax.Precision.HIGHEST


def diffuse(padded, wet_pad, forcing, diffusivity):
    centre = padded[:, 1:-1, 1:-1]
    span_rows = centre.shape[1]
    span_cols = centre.shape[2]
    laplace_sum = jnp.zeros_like(centre)
    for row_from, col_from in ((0, 1), (2, 1), (1, 0), (1, 2)):
        neighbour = padded[:, row_from:row_from + span_rows, col_from:col_from + span_cols]
        neighbour_wet = wet_pad[row_from:row_from + span_rows, col_from:col_from + span_cols]
        laplace_sum = laplace_sum + neighbour_wet * (neighbour - centre)
    return centre + wet_pad[1:-1, 1:-1] * (diffusivity[:, None, None] * laplace_sum + forcing)


def tile_solve(inverses, columns):
    tiles = columns.reshape(NVAR, K, N_ATM, N_OCN * COL_DEV)
    solved = jnp.einsum('avkj,vjac->vkac', inverses, tiles, precision=highest)
    return solved.reshape(NVAR, K, NCOLS)


def reference(atmos_state, inverses, flux_weight, surface_weight, area_table, xc_column, xc_dest, xc_cell, xc_class, tracer, land_sea, forcing_weight, surface_map, diffusivity):
    diffused = tile_solve(inverses, atmos_state)
    flux_rows = jnp.einsum('vkc,vkf->cf', diffused, flux_weight, precision=highest)
    cell_area = area_table[xc_class]
    positions = jnp.arange(XCELLS, dtype=jnp.int32)
    global_column = (positions // XC_DEV) * COL_DEV + xc_column
    cell_rows = (cell_area[:, None] * flux_rows[global_column]).astype(jnp.bfloat16)
    target = xc_dest[:, 0]
    tile_row = target // N_OCN
    tile_col = target % N_OCN
    ocean_cell = (tile_row * OY + xc_cell // OX) * NX + tile_col * OX + xc_cell % OX
    forcing_rows = jnp.zeros((NY * NX, FLUX), jnp.float32).at[ocean_cell].add(cell_rows.astype(jnp.float32))
    forcing = jnp.einsum('lf,cf->lc', forcing_weight, forcing_rows, precision=highest).reshape(L, NY, NX)
    wet_cells = land_sea.astype(jnp.float32)
    wet_pad = jnp.pad(wet_cells, 1)
    current = tracer
    for substep in range(OSTEPS):
        padded = jnp.pad(current, ((0, 0), (1, 1), (1, 1)))
        current = diffuse(padded, wet_pad, forcing, diffusivity)
    surface = jnp.einsum('lc,lf->cf', current.reshape(L, NY * NX), surface_map, precision=highest).astype(jnp.bfloat16)
    contrib = cell_area[:, None] * surface[ocean_cell].astype(jnp.float32)
    surface_sum = jnp.zeros((NCOLS, FLUX), jnp.float32).at[global_column].add(contrib)
    surface_tend = jnp.einsum('vkf,cf->vkc', surface_weight, surface_sum, precision=highest)
    final_state = tile_solve(inverses, diffused + surface_tend)
    return final_state, current
```

```python
import functools
import jax
import jax.numpy as jnp
from jax import lax
from jax.experimental import pallas as pl
from jax.experimental.pallas import tpu as pltpu
from jax.sharding import PartitionSpec as P

OSTEPS = 4
OY = 32
OX = 128
OCELLS = OY * OX
STRIPS = 8
f32 = jnp.float32
bf16 = jnp.bfloat16
i32 = jnp.int32


def nn(a, b):
    return jnp.dot(a, b, preferred_element_type=f32)


def nt(a, b):
    return lax.dot_general(a, b, (((1,), (1,)), ((), ())), preferred_element_type=f32)


def split(x):
    high = x.astype(bf16)
    return high, (x - high.astype(f32)).astype(bf16)


def three(dot, a, b):
    ah, al = split(a)
    bh, bl = split(b)
    return dot(ah, bh) + dot(ah, bl) + dot(al, bh)


def iota(shape, dim):
    return lax.broadcasted_iota(i32, shape, dim)


def flat(x):
    return jnp.concatenate([x[i : i + 1, :] for i in range(x.shape[0])], axis=1)


def onehot(row, size):
    return jnp.where(iota((size, row.shape[1]), 0) == row, 1.0, 0.0).astype(bf16)


def place(high, low, payloads, rows):
    lines = iota((rows, high.shape[1]), 0) == high
    left = jnp.concatenate([jnp.where(lines, p, 0.0) for p in payloads], axis=0).astype(bf16)
    out = nt(left, onehot(low, 128))
    return [out[i * rows : (i + 1) * rows] for i in range(len(payloads))]


def stacked(x):
    return jnp.concatenate([x[:, h : h + 256] for h in range(0, x.shape[1], 256)], axis=0)


def gather(source, low, high, width, chunk=512):
    count = source.shape[0] // width
    outs = []
    for start in range(0, low.shape[1], chunk):
        stop = min(start + chunk, low.shape[1])
        part = nn(source, onehot(low[:, start:stop], 256))
        hc = high[:, start:stop]
        total = jnp.where(hc == 0, part[:width], 0.0)
        for h in range(1, count):
            total = jnp.where(hc == h, part[h * width : (h + 1) * width], total)
        outs.append(total)
    return outs[0] if len(outs) == 1 else jnp.concatenate(outs, axis=1)


def pick(level_rows, lane_rows, base):
    index = iota(level_rows.shape, 0)
    for i, row in enumerate(lane_rows):
        level_rows = jnp.where(index == base + i, row, level_rows)
    return level_rows


def roll(x, shift):
    shift = shift % 128
    return x if shift == 0 else pltpu.roll(x, shift, 1)


def row_of(x, y):
    return x[:, y * OX : (y + 1) * OX]


def border_block(x, lane):
    blocks = []
    for i in range(2):
        block = jnp.zeros((x.shape[0], OX), f32)
        for b in range(4):
            for j in range(4):
                first = b * 32 + j * 8
                moved = roll(row_of(x, b * 8 + i * 4 + j), first + 4)
                block = jnp.where((lane >= first) & (lane < first + 8), moved, block)
        blocks.append(block)
    return jnp.concatenate(blocks, axis=1)


def strips(x, halo, lane):
    outs = []
    for j in range(STRIPS):
        side = roll(row_of(halo, j // 4), 8 - (j % 4) * 8)
        for b in range(4):
            line = row_of(x, b * 8 + j)
            first = b * 32
            side = jnp.where((lane >= first) & (lane < first + 8), roll(line, first + 8), side)
            side = jnp.where(
                (lane >= first + 16) & (lane < first + 24), roll(line, first + 16), side
            )
        outs.append(side)
    return outs


def send_kernel(
    peers, levels, width, borders,
    area_ref, col_ref, dest_ref, cell_ref, class_ref, inv_ref, flux_ref, fw_ref, state_ref,
    tracer_ref, land_ref,
    packed_ref, *rest,
):
    side_refs = rest[: len(borders)]
    forcing_ref, t_ref, omap_ref, oarea_ref, smap_ref, sarea_ref, fw_pad = rest[len(borders) :]
    me = lax.axis_index("ocn")
    slots = packed_ref.shape[1]
    slot_rows = slots // 128
    slot_pad = -(-slot_rows // 8) * 8
    lines = col_ref.shape[0]
    lane = iota((1, 128), 1)

    offset = (dest_ref[...] - me) & (peers - 1)
    cells = cell_ref[...]
    classes = class_ref[...]
    cols = col_ref[...]
    area = jnp.zeros(cols.shape, f32)
    for i in range(area_ref.shape[0]):
        area = jnp.where(classes == i, area_ref[i], area)

    hits = [jnp.where(offset == k, 1.0, 0.0) for k in range(1, peers)]
    hot = jnp.concatenate(hits, axis=0)
    upper = jnp.where(iota((128, 128), 0) <= iota((128, 128), 1), 1.0, 0.0).astype(bf16)
    running = nn(hot.astype(bf16), upper)
    count = running.shape[0]
    totals = jnp.broadcast_to(running[:, 127:128], running.shape).astype(bf16)
    below = jnp.where(iota((count, count), 1) < iota((count, count), 0), 1.0, 0.0).astype(bf16)
    before = nn(below, totals)
    place_of = running + before - 1.0
    slot = jnp.full(cols.shape, -1.0, f32)
    for k in range(1, peers):
        at = (k - 1) * lines
        slot = jnp.where(offset == k, place_of[at : at + lines], slot)
    slot = slot.astype(i32)
    position = iota((slot_pad, 128), 0) * 128 + iota((slot_pad, 128), 1)
    segment = jnp.full((slot_pad, 128), 1, i32)
    for k in range(2, peers):
        at = (k - 1) * lines
        start = before[at : at + 1, :].astype(i32)
        segment = segment + jnp.where(position >= start, 1, 0)

    a1 = area.astype(bf16).astype(f32)
    a2 = (area - a1).astype(bf16).astype(f32)
    a3 = area - a1 - a2
    slot_f, cell_f = flat(slot), flat(cells)
    col_f = flat(cols)
    areas = [flat(a1), flat(a2), flat(a3)]
    col_low = (col_f & 255).astype(f32)
    col_high = lax.shift_right_arithmetic(col_f, 8).astype(f32)
    cell_low = cell_f & 127
    cell_high = lax.shift_right_arithmetic(cell_f, 7)
    got = place(
        lax.shift_right_arithmetic(slot_f, 7), slot_f & 127,
        [col_low, col_high] + areas + [cell_high.astype(f32), cell_low.astype(f32)], slot_pad,
    )
    keep = [flat(g[:slot_rows]) for g in got]
    s_low, s_high = keep[0].astype(i32), keep[1].astype(i32)
    s_area = keep[2] + keep[3] + keep[4]
    smap_ref[0:1, :] = s_low
    smap_ref[1:2, :] = s_high
    smap_ref[2:3, :] = flat(segment[:slot_rows])
    sarea_ref[...] = s_area

    local_high = jnp.where(flat(offset) == 0, cell_high, -1)
    own = place(local_high, cell_low, [col_low, col_high + 1.0] + areas, OY)
    o_low, o_high = own[0].astype(i32), own[1].astype(i32) - 1
    o_area = own[2] + own[3] + own[4]
    omap_ref[0:1, :] = flat(o_low)
    omap_ref[1:2, :] = flat(o_high)
    oarea_ref[...] = flat(o_area)

    blank = jnp.zeros((2, 128), f32)
    edge = []
    for m in (own[0], own[1], o_area):
        block = blank
        for b in range(4):
            part = m[b * 8 : (b + 1) * 8]
            for j in range(4):
                first = b * 32 + j * 8
                moved = roll(part, first + 4)
                pair = jnp.concatenate([moved[j : j + 1], moved[4 + j : 5 + j]], axis=0)
                block = jnp.where((lane >= first) & (lane < first + 8), pair, block)
        edge.append(flat(block))

    fw_pad[...] = jnp.zeros_like(fw_pad)
    fw_pad[0:levels, :] = fw_ref[...]
    fw = fw_pad[...]
    forcing = None
    for v in range(flux_ref.shape[0]):
        pulled = three(nn, three(nt, fw, flux_ref[v]), inv_ref[0, v])
        term = three(nn, pulled, state_ref[v])
        forcing = term if forcing is None else forcing + term
    forcing = forcing.astype(bf16)
    forcing_ref[...] = forcing
    source = stacked(forcing)

    for y in range(OY):
        at = pl.ds(y * OX, OX)
        t_ref[0:levels, at] = tracer_ref[pl.ds(y, levels, stride=OY), :]
        t_ref[levels : levels + 1, at] = land_ref[y : y + 1, :].astype(f32)
        t_ref[levels + 1 : width, at] = jnp.zeros((width - levels - 1, OX), f32)

    rows = gather(source, s_low, s_high, width) * s_area
    rows = pick(rows, keep[5:7], levels + 1).astype(bf16)
    packed_ref[...] = rows
    f_edge = gather(source, edge[0].astype(i32), edge[1].astype(i32) - 1, width) * edge[2]
    t_edge = border_block(t_ref[...], lane)
    lead = (lane & 7) < 4
    to_right, to_left = [], []
    for i in range(2):
        fe, te = row_of(f_edge, i), row_of(t_edge, i)
        to_right.append(jnp.where(lead, fe, roll(te, 4)))
        to_left.append(jnp.where(lead, roll(fe, -4), te))
    to_right = jnp.concatenate(to_right, axis=1)
    to_left = jnp.concatenate(to_left, axis=1)
    for mask, ref in zip(borders, side_refs):
        ref[:, 0:slots] = rows
        ref[:, slots : slots + 256] = jnp.where((me ^ mask) == me + 1, to_right, to_left).astype(
            bf16
        )


def local_kernel(width, forcing_ref, omap_ref, oarea_ref, out_ref):
    source = stacked(forcing_ref[...])
    out_ref[...] = gather(source, omap_ref[0:1, :], omap_ref[1:2, :], width) * oarea_ref[...]


def receive_kernel(peers, levels, width, borders, packed_ref, smap_ref, local_ref, t_ref, *rest):
    got = rest[: peers - 1]
    f_ref, fs_ref, ts_ref, cmap_ref, even_ref, odd_ref = rest[peers - 1 :]
    me = lax.axis_index("ocn")
    slots = packed_ref.shape[1]
    lane = iota((1, 128), 1)
    segment = smap_ref[2:3, :]
    chunks = slots // 256

    def meant_for(tile):
        total = jnp.zeros((width, slots), f32)
        for mask in range(peers):
            ref = packed_ref if mask == 0 else got[mask - 1]
            step = (tile - (me ^ mask)) & (peers - 1)
            total = jnp.where(segment == step, ref[:, 0:slots].astype(f32), total)
        high = total[levels + 1 : levels + 2, :].astype(i32)
        low = total[levels + 2 : levels + 3, :].astype(i32)
        return stacked(total.astype(bf16)), high, low

    index = iota((1, slots), 1)
    payload = [(index & 255).astype(f32), (lax.shift_right_arithmetic(index, 8) + 1).astype(f32)]

    source, high, low = meant_for(me)
    cell = high * 128 + low
    cmap_ref[0:1, :] = cell & 255
    cmap_ref[1:2, :] = lax.shift_right_arithmetic(cell, 8)
    where_low, where_high = place(high, low, payload, OY)
    f_ref[...] = local_ref[...] + gather(
        source, flat(where_low).astype(i32), flat(where_high).astype(i32) - 1, width
    )

    halo_f = None
    for step in (-1, 1):
        source, high, low = meant_for(me + step)
        at = low - 120 if step < 0 else low
        inside = (low >= 124) if step < 0 else (low < 4)
        block = lax.shift_right_arithmetic(high & 7, 2)
        spot = lax.shift_right_arithmetic(high, 3) * 32 + (high & 3) * 8 + at
        where_low, where_high = place(jnp.where(inside, block, -1), spot, payload, 8)
        part = gather(
            source, flat(where_low[:2]).astype(i32), flat(where_high[:2]).astype(i32) - 1, width
        )
        halo_f = part if halo_f is None else halo_f + part

    def side_from(tile):
        block = jnp.zeros((width, 256), f32)
        for mask in borders:
            block = jnp.where(
                (me ^ mask) == tile, got[mask - 1][:, slots : slots + 256].astype(f32), block
            )
        return block

    from_left, from_right = side_from(me - 1), side_from(me + 1)
    lead = (lane & 7) < 4
    side_f, side_t = [], []
    for i in range(2):
        fl, fr = row_of(from_left, i), row_of(from_right, i)
        side_f.append(jnp.where(lead, fr, roll(fl, 4)) + row_of(halo_f, i))
        side_t.append(jnp.where(lead, roll(fr, -4), fl))
    f_strips = strips(f_ref[...], jnp.concatenate(side_f, axis=1), lane)
    t_strips = strips(t_ref[...], jnp.concatenate(side_t, axis=1), lane)
    for j in range(STRIPS):
        fs_ref[:, j * OX : (j + 1) * OX] = f_strips[j]
        ts_ref[:, j * OX : (j + 1) * OX] = t_strips[j]

    def corner(parts, top):
        block = jnp.zeros((width, OX), f32)
        for m in range(4):
            inside = (lane >= m * 32) & (lane < m * 32 + 32)
            moved = roll(parts[m], 32 * m) if top else roll(parts[4 + m], 32 * (m - 3))
            block = jnp.where(inside, moved, block)
        return block

    top = jnp.concatenate(
        [f_ref[:, 0 : 3 * OX], corner(f_strips, True), t_ref[:, 0 : 4 * OX],
         corner(t_strips, True)], axis=1,
    )
    bottom = jnp.concatenate(
        [f_ref[:, 29 * OX : 32 * OX], corner(f_strips, False), t_ref[:, 28 * OX : 32 * OX],
         corner(t_strips, False)], axis=1,
    )
    is_even = (lax.axis_index("atm") & 1) == 0
    even_ref[...] = jnp.where(is_even, bottom, top).astype(bf16)
    odd_ref[...] = jnp.where(is_even, top, bottom).astype(bf16)


def ocean_kernel(
    levels, width,
    f_ref, fs_ref, t_ref, ts_ref, even_ref, odd_ref, dif_ref, cmap_ref,
    out_ref, tt_ref, back_ref,
    s, fx, ss, fsx, w8, n8, ws8, ns8, d8,
):
    row = lax.axis_index("atm")
    me = lax.axis_index("ocn")
    rows_atm = lax.axis_size("atm")
    peers = lax.axis_size("ocn")
    is_even = (row & 1) == 0
    lane = iota((1, 128), 1)
    block = lax.shift_right_arithmetic(lane, 5)
    even, odd = even_ref[...].astype(f32), odd_ref[...].astype(f32)
    top = jnp.where(is_even, odd, even)
    bottom = jnp.where(is_even, even, odd)
    spot = lane & 31
    outside = ((me == 0) & (spot >= 12) & (spot < 16)) | (
        (me == peers - 1) & (spot >= 8) & (spot < 12)
    )
    top_wet = jnp.where(row > 0, top[levels : levels + 1, 512:1152], 0.0)
    bottom_wet = jnp.where(row < rows_atm - 1, bottom[levels : levels + 1, 512:1152], 0.0)
    main_wet = t_ref[levels : levels + 1, :]
    rows_all = OY + 8
    w8[:, 0 : 4 * OX] = jnp.broadcast_to(top_wet[:, 0:512], (8, 512))
    w8[:, 4 * OX : 36 * OX] = jnp.broadcast_to(main_wet, (8, OCELLS))
    w8[:, 36 * OX : 40 * OX] = jnp.broadcast_to(bottom_wet[:, 0:512], (8, 512))
    for j in range(STRIPS + 2):
        if j == 0:
            line = top_wet[:, 512:640]
        elif j == STRIPS + 1:
            line = bottom_wet[:, 512:640]
        else:
            line = ts_ref[levels : levels + 1, (j - 1) * OX : j * OX]
        ws8[:, j * OX : (j + 1) * OX] = jnp.broadcast_to(jnp.where(outside, 0.0, line), (8, OX))

    def at(ref, y):
        return ref[:, y * OX : (y + 1) * OX]

    def ends(parts, j):
        if j == 0:
            return roll(parts[0], 32), roll(jnp.where(block == 0, parts[1], parts[0]), 96)
        if j == 1:
            return roll(jnp.where(block == 3, parts[0], parts[STRIPS]), 32), parts[2]
        if j == STRIPS:
            return parts[STRIPS - 1], roll(
                jnp.where(block == 0, parts[STRIPS + 1], parts[1]), 96
            )
        if j == STRIPS + 1:
            return roll(jnp.where(block == 3, parts[STRIPS], parts[j]), 32), roll(parts[j], 96)
        return parts[j - 1], parts[j + 1]

    for y in range(1, rows_all - 1):
        here = at(w8, y)
        n8[:, y * OX : (y + 1) * OX] = (
            at(w8, y - 1) + at(w8, y + 1) + roll(here, 1) + roll(here, -1)
        )
    parts = [at(ws8, j) for j in range(STRIPS + 2)]
    for j in range(STRIPS + 2):
        up, down = ends(parts, j)
        ns8[:, j * OX : (j + 1) * OX] = up + down + roll(parts[j], 1) + roll(parts[j], -1)

    diag = iota((width, levels), 0) == iota((width, levels), 1)
    column = jnp.sum(jnp.where(diag, dif_ref[...], 0.0), axis=1, keepdims=True)
    d8[...] = jnp.broadcast_to(column, (width, OX))

    fx[:, OX : 4 * OX] = top[:, 0:384]
    fx[:, 4 * OX : 36 * OX] = f_ref[...]
    fx[:, 36 * OX : 39 * OX] = bottom[:, 0:384]
    fsx[:, 0:OX] = top[:, 384:512]
    fsx[:, OX : 9 * OX] = fs_ref[...]
    fsx[:, 9 * OX : 10 * OX] = bottom[:, 384:512]
    s[:, 0 : 4 * OX] = top[:, 512:1024] * w8[0:1, 0 : 4 * OX]
    s[:, 4 * OX : 36 * OX] = t_ref[...] * w8[0:1, 4 * OX : 36 * OX]
    s[:, 36 * OX : 40 * OX] = bottom[:, 512:1024] * w8[0:1, 36 * OX : 40 * OX]
    ss[:, 0:OX] = top[:, 1024:1152] * ws8[0:1, 0:OX]
    ss[:, OX : 9 * OX] = ts_ref[...] * ws8[0:1, OX : 9 * OX]
    ss[:, 9 * OX : 10 * OX] = bottom[:, 1024:1152] * ws8[0:1, 9 * OX : 10 * OX]

    def group(g, carry):
        lev = pl.ds(pl.multiple_of(g * 8, 8), 8)

        def load(ref, y):
            return ref[lev, y * OX : (y + 1) * OX]

        dif = d8[lev, :]
        for step in range(OSTEPS):
            before, here = load(s, step), load(s, step + 1)
            for y in range(step + 1, rows_all - 1 - step):
                after = load(s, y + 1)
                lap = before + after + roll(here, 1) + roll(here, -1) - at(n8, y) * here
                s[lev, y * OX : (y + 1) * OX] = here + at(w8, y) * (dif * lap + load(fx, y))
                before, here = here, after
        now = [load(ss, j) for j in range(STRIPS + 2)]
        for step in range(OSTEPS):
            new = []
            for j in range(STRIPS + 2):
                up, down = ends(now, j)
                here = now[j]
                lap = up + down + roll(here, 1) + roll(here, -1) - at(ns8, j) * here
                new.append(here + at(ws8, j) * (dif * lap + load(fsx, j)))
            now = new
        for y in range(OY):
            b, j = y // 8, y % 8
            line = now[j + 1]
            value = load(s, y + 4)
            value = jnp.where(lane < 4, roll(line, -(b * 32 + 16)), value)
            value = jnp.where(lane >= 124, roll(line, 120 - b * 32), value)
            tt_ref[lev, y * OX : (y + 1) * OX] = jnp.where(
                at(w8, y + 4) > 0.0, value, load(t_ref, y)
            )
        return carry

    lax.fori_loop(0, width // 8, group, 0)
    for y in range(OY):
        out_ref[pl.ds(y, levels, stride=OY), :] = tt_ref[0:levels, y * OX : (y + 1) * OX]
    source = stacked(tt_ref[...].astype(bf16))
    back_ref[...] = gather(source, cmap_ref[0:1, :], cmap_ref[1:2, :], width).astype(bf16)


def state_kernel(levels, width, inv_ref, sw_ref, sm_ref, state_ref, out_ref, h_ref, sm_pad, high, low):
    vars_, size = inv_ref.shape[1], inv_ref.shape[2]

    @pl.when(pl.program_id(0) == 0)
    def _():
        sm_pad[...] = jnp.zeros_like(sm_pad)
        sm_pad[0:levels, :] = sm_ref[...]
        for v in range(vars_):
            inv = inv_ref[0, v]
            h_ref[v] = three(nn, inv, three(nt, sw_ref[v], sm_pad[...]))
            high[v], low[v] = split(three(nn, inv, inv))

    for v in range(vars_):
        sh, sl = split(state_ref[v])
        out_ref[v] = nn(high[v], sh) + nn(high[v], sl) + nn(low[v], sh)


def sum_kernel(width, tt_ref, omap_ref, oarea_ref, out_ref):
    count = out_ref.shape[1] // 256
    chunk = 1024
    total = None
    for start in range(0, OCELLS, chunk):
        value = tt_ref[:, start : start + chunk] * oarea_ref[:, start : start + chunk]
        high = omap_ref[1:2, start : start + chunk]
        left = jnp.concatenate(
            [jnp.where(high == h, value, 0.0) for h in range(count)], axis=0
        ).astype(bf16)
        part = nt(left, onehot(omap_ref[0:1, start : start + chunk], 256))
        total = part if total is None else total + part
    for h in range(count):
        out_ref[:, h * 256 : (h + 1) * 256] = total[h * width : (h + 1) * width]


def final_kernel(
    peers, width, smap_ref, sarea_ref, sum_ref, h_ref, base_ref, *rest
):
    got = rest[: peers - 1]
    out_ref, value = rest[peers - 1 :]
    step = pl.program_id(0)
    columns = sum_ref.shape[1]
    count = columns // 256

    @pl.when(step == 0)
    def _():
        me = lax.axis_index("ocn")
        segment = smap_ref[2:3, :]
        total = jnp.zeros(value.shape, f32)
        for mask in range(1, peers):
            offset = ((me ^ mask) - me) & (peers - 1)
            total = jnp.where(segment == offset, got[mask - 1][...].astype(f32), total)
        value[...] = total * sarea_ref[...]

    back = value[...]
    high = smap_ref[1:2, :] - step * count
    left = jnp.concatenate(
        [jnp.where(high == h, back, 0.0) for h in range(count)], axis=0
    ).astype(bf16)
    part = nt(left, onehot(smap_ref[0:1, :], 256))
    sums = jnp.concatenate([part[h * width : (h + 1) * width] for h in range(count)], axis=1)
    sums = sums + sum_ref[...]
    sh, sl = split(sums)
    for v in range(out_ref.shape[0]):
        hh, hl = split(h_ref[v])
        out_ref[v] = base_ref[v] + (nn(hh, sh) + nn(hh, sl) + nn(hl, sh))


def on_device(
    atmos_state, inverses, flux_weight, surface_weight, area_table, xc_column, xc_dest, xc_cell,
    xc_class, tracer, land_sea, forcing_weight, surface_map, diffusivity,
):
    peers, tiles = lax.axis_size("ocn"), lax.axis_size("atm")
    vars_, size, columns = atmos_state.shape
    cells = xc_column.shape[0]
    levels = tracer.shape[0]
    slots = cells - 3 * cells // peers
    width = -(-(levels + 3) // 16) * 16
    borders = sorted({i ^ (i + 1) for i in range(peers - 1)})
    sds = jax.ShapeDtypeStruct
    params = pltpu.CompilerParams(vmem_limit_bytes=56 * 1024 * 1024)
    smem = pl.BlockSpec(memory_space=pltpu.SMEM)
    vmem = pl.BlockSpec(memory_space=pltpu.VMEM)

    def swap(x, axis, pairs):
        return lax.ppermute(x, axis, pairs)

    def xor_swap(x, mask):
        return swap(x, "ocn", [(i, i ^ mask) for i in range(peers)])

    grid_of = lambda x: x.reshape(cells // 128, 128)
    outs = pl.pallas_call(
        functools.partial(send_kernel, peers, levels, width, borders),
        out_shape=[sds((width, slots), bf16)]
        + [sds((width, slots + 256), bf16)] * len(borders)
        + [
            sds((width, columns), bf16), sds((width, OCELLS), f32), sds((2, OCELLS), i32),
            sds((1, OCELLS), f32), sds((3, slots), i32), sds((1, slots), f32),
        ],
        in_specs=[smem] + [vmem] * 10,
        out_specs=[vmem] * (7 + len(borders)),
        scratch_shapes=[pltpu.VMEM((width, forcing_weight.shape[1]), f32)],
        compiler_params=params,
        name="send",
    )(
        area_table, grid_of(xc_column), grid_of(xc_dest), grid_of(xc_cell), grid_of(xc_class),
        inverses, flux_weight, forcing_weight, atmos_state,
        tracer.reshape(levels * OY, OX), land_sea,
    )
    packed, sides = outs[0], outs[1 : 1 + len(borders)]
    forcing_cols, t0, omap, oarea, smap, sarea = outs[1 + len(borders) :]
    got = []
    for mask in range(1, peers):
        buffer = sides[borders.index(mask)] if mask in borders else packed
        got.append(xor_swap(buffer, mask))

    local = pl.pallas_call(
        functools.partial(local_kernel, width),
        out_shape=sds((width, OCELLS), f32),
        in_specs=[vmem] * 3, out_specs=vmem, compiler_params=params, name="local",
    )(forcing_cols, omap, oarea)

    send_rows = 4 * OX + OX + 4 * OX
    f_all, fs, ts, cmap, even, odd = pl.pallas_call(
        functools.partial(receive_kernel, peers, levels, width, borders),
        out_shape=[
            sds((width, OCELLS), f32), sds((width, STRIPS * OX), f32),
            sds((width, STRIPS * OX), f32), sds((2, slots), i32),
            sds((width, send_rows), bf16), sds((width, send_rows), bf16),
        ],
        in_specs=[vmem] * (3 + peers), out_specs=[vmem] * 6, compiler_params=params,
        name="receive",
    )(packed, smap, local, t0, *got)

    first = [(i, i ^ 1) for i in range(tiles)]
    second = [(i, (i + 1) % tiles if i & 1 else (i - 1) % tiles) for i in range(tiles)]
    even, odd = swap(even, "atm", first), swap(odd, "atm", second)

    block = 512
    base, back_map = pl.pallas_call(
        functools.partial(state_kernel, levels, width),
        out_shape=[sds((vars_, size, columns), f32), sds((vars_, size, width), f32)],
        grid=(columns // block,),
        in_specs=[
            pl.BlockSpec(inverses.shape, lambda i: (0, 0, 0, 0)),
            pl.BlockSpec(surface_weight.shape, lambda i: (0, 0, 0)),
            pl.BlockSpec(surface_map.shape, lambda i: (0, 0)),
            pl.BlockSpec((vars_, size, block), lambda i: (0, 0, i)),
        ],
        out_specs=[
            pl.BlockSpec((vars_, size, block), lambda i: (0, 0, i)),
            pl.BlockSpec((vars_, size, width), lambda i: (0, 0, 0)),
        ],
        scratch_shapes=[
            pltpu.VMEM((width, surface_map.shape[1]), f32),
            pltpu.VMEM((vars_, size, size), bf16), pltpu.VMEM((vars_, size, size), bf16),
        ],
        compiler_params=params, name="state",
    )(inverses, surface_weight, surface_map, atmos_state)

    long = (OY + 8) * OX
    thin = (STRIPS + 2) * OX
    tracer_out, t4, back = pl.pallas_call(
        functools.partial(ocean_kernel, levels, width),
        out_shape=[
            sds((levels * OY, OX), f32), sds((width, OCELLS), f32), sds((width, slots), bf16),
        ],
        in_specs=[vmem] * 8, out_specs=[vmem] * 3,
        scratch_shapes=[
            pltpu.VMEM((width, long), f32), pltpu.VMEM((width, long), f32),
            pltpu.VMEM((width, thin), f32), pltpu.VMEM((width, thin), f32),
            pltpu.VMEM((8, long), f32), pltpu.VMEM((8, long), f32),
            pltpu.VMEM((8, thin), f32), pltpu.VMEM((8, thin), f32),
            pltpu.VMEM((width, OX), f32),
        ],
        compiler_params=params, name="ocean",
    )(f_all, fs, t0, ts, even, odd, diffusivity.reshape(1, levels), cmap)

    returned = [xor_swap(back, mask) for mask in range(1, peers)]
    sums = pl.pallas_call(
        functools.partial(sum_kernel, width),
        out_shape=sds((width, columns), f32),
        in_specs=[vmem] * 3, out_specs=vmem, compiler_params=params, name="sum",
    )(t4, omap, oarea)

    final_state = pl.pallas_call(
        functools.partial(final_kernel, peers, width),
        out_shape=sds((vars_, size, columns), f32),
        grid=(columns // block,),
        in_specs=[
            pl.BlockSpec(smap.shape, lambda i: (0, 0)),
            pl.BlockSpec(sarea.shape, lambda i: (0, 0)),
            pl.BlockSpec((width, block), lambda i: (0, i)),
            pl.BlockSpec(back_map.shape, lambda i: (0, 0, 0)),
            pl.BlockSpec((vars_, size, block), lambda i: (0, 0, i)),
        ]
        + [pl.BlockSpec((width, slots), lambda i: (0, 0))] * (peers - 1),
        out_specs=pl.BlockSpec((vars_, size, block), lambda i: (0, 0, i)),
        scratch_shapes=[pltpu.VMEM((width, slots), f32)],
        compiler_params=params, name="final",
    )(smap, sarea, sums, back_map, base, *returned)
    return (final_state, tracer_out.reshape(tracer.shape))


def solution(mesh):
    in_specs = (
        P(None, None, ("member", "atm", "ocn")),
        P("atm", None, None, None),
        P(),
        P(),
        P(),
        P(("atm", "ocn")),
        P(("atm", "ocn"), None),
        P(("atm", "ocn")),
        P(("atm", "ocn")),
        P(None, "atm", ("member", "ocn")),
        P("atm", "ocn"),
        P(),
        P(),
        P(),
    )
    out_specs = (P(None, None, ("member", "atm", "ocn")), P(None, "atm", ("member", "ocn")))
    return jax.shard_map(
        on_device, mesh=mesh, in_specs=in_specs, out_specs=out_specs, check_vma=False
    )
```

```python
import functools
import jax
import jax.numpy as jnp
from jax import lax
from jax.experimental import pallas as pl
from jax.experimental.pallas import tpu as pltpu
from jax.sharding import PartitionSpec as P

OSTEPS = 4
NVAR = 4
OY = 32
OX = 128
OCELLS = OY * OX
STRIPS = 8
f32 = jnp.float32
bf16 = jnp.bfloat16
i32 = jnp.int32


def nn(a, b):
    return jnp.dot(a, b, preferred_element_type=f32)


def nt(a, b):
    return lax.dot_general(a, b, (((1,), (1,)), ((), ())), preferred_element_type=f32)


def split(x):
    high = x.astype(bf16)
    return high, (x - high.astype(f32)).astype(bf16)


def three(dot, a, b):
    ah, al = split(a)
    bh, bl = split(b)
    return dot(ah, bh) + dot(ah, bl) + dot(al, bh)


def doubled(x):
    return jnp.concatenate(list(split(x)), axis=0)


def wide(left, right, dot=nn):
    count = left.shape[0] // 2
    high, low = split(right)
    both = dot(left, high)
    return both[:count] + both[count:] + dot(left[:count], low)


def column_block(ref, var, first, blocks):
    size, rows, lanes = ref.shape
    lines = ref.reshape(size * rows, lanes)
    step = NVAR
    return jnp.concatenate(
        [lines[pl.ds((first + i) * step + var, size, stride=rows), :] for i in range(blocks)],
        axis=1,
    )


def iota(shape, dim):
    return lax.broadcasted_iota(i32, shape, dim)


def flat(x):
    return jnp.concatenate([x[i : i + 1, :] for i in range(x.shape[0])], axis=1)


def onehot(row, size):
    return jnp.where(iota((size, row.shape[1]), 0) == row, 1.0, 0.0).astype(bf16)


def place(high, low, payloads, rows):
    lines = iota((rows, high.shape[1]), 0) == high
    left = jnp.concatenate([jnp.where(lines, p, 0.0) for p in payloads], axis=0).astype(bf16)
    out = nt(left, onehot(low, 128))
    return [out[i * rows : (i + 1) * rows] for i in range(len(payloads))]


def stacked(x):
    return jnp.concatenate([x[:, h : h + 256] for h in range(0, x.shape[1], 256)], axis=0)


def two_terms(ref):
    return jnp.concatenate([stacked(ref[0]), stacked(ref[1])], axis=1)


def gather(source, low, high, width, chunk=512):
    count = source.shape[0] // width
    outs = []
    for start in range(0, low.shape[1], chunk):
        stop = min(start + chunk, low.shape[1])
        hot = onehot(low[:, start:stop], 256)
        if source.shape[1] == 512:
            hot = jnp.concatenate([hot, hot], axis=0)
        part = nn(source, hot)
        hc = high[:, start:stop]
        total = jnp.where(hc == 0, part[:width], 0.0)
        for h in range(1, count):
            total = jnp.where(hc == h, part[h * width : (h + 1) * width], total)
        outs.append(total)
    return outs[0] if len(outs) == 1 else jnp.concatenate(outs, axis=1)


def spread(value, low, high, count):
    vh, vl = split(value)
    hot = onehot(low, 256)
    outs = []
    for term in (vh, vl):
        parts = [jnp.where(high == h, term.astype(f32), 0.0) for h in range(count)]
        outs.append(nt(jnp.concatenate(parts, axis=0).astype(bf16), hot))
    return outs[0] + outs[1]


def pick(level_rows, lane_rows, base):
    index = iota(level_rows.shape, 0)
    for i, row in enumerate(lane_rows):
        level_rows = jnp.where(index == base + i, row, level_rows)
    return level_rows


def roll(x, shift):
    shift = shift % 128
    return x if shift == 0 else pltpu.roll(x, shift, 1)


def row_of(x, y):
    return x[:, y * OX : (y + 1) * OX]


def border_block(x, lane):
    blocks = []
    for i in range(2):
        block = jnp.zeros((x.shape[0], OX), f32)
        for b in range(4):
            for j in range(4):
                first = b * 32 + j * 8
                moved = roll(row_of(x, b * 8 + i * 4 + j), first + 4)
                block = jnp.where((lane >= first) & (lane < first + 8), moved, block)
        blocks.append(block)
    return jnp.concatenate(blocks, axis=1)


def strips(x, halo, lane):
    outs = []
    for j in range(STRIPS):
        side = roll(row_of(halo, j // 4), 8 - (j % 4) * 8)
        for b in range(4):
            line = row_of(x, b * 8 + j)
            first = b * 32
            side = jnp.where((lane >= first) & (lane < first + 8), roll(line, first + 8), side)
            side = jnp.where(
                (lane >= first + 16) & (lane < first + 24), roll(line, first + 16), side
            )
        outs.append(side)
    return outs


def send_kernel(
    peers, levels, width, borders,
    *refs,
):
    sources, rest = refs[:11], refs[11:]
    packed_ref, rest = rest[0], rest[1:]
    side_refs, rest = rest[: len(borders)], rest[len(borders) :]
    (even_ref, odd_ref), rest = rest[:2], rest[2:]
    forcing_ref, t_ref, omap_ref, oarea_ref, smap_ref, sarea_ref, state_ref = rest[:7]
    staged, fw_pad, sems, state_sems = rest[7:17], rest[17], rest[18], rest[19]
    (area_ref, col_ref, dest_ref, cell_ref, class_ref, inv_ref, flux_ref, fw_ref, tracer_ref,
     land_ref) = staged
    loads = [
        pltpu.make_async_copy(a, b, sems.at[i])
        for i, (a, b) in enumerate(zip(sources[:10], staged))
    ]
    for load in loads:
        load.start()
    state_hbm = sources[10]
    parts = state_sems.shape[0]
    part_rows = state_ref.shape[1] // parts
    state_loads = []
    for i in range(parts):
        at = pl.ds(i * part_rows, part_rows)
        state_loads.append(
            pltpu.make_async_copy(
                state_hbm.at[:, at, :], state_ref.at[:, at, :], state_sems.at[i]
            )
        )
        state_loads[i].start()
    for load in loads[:5]:
        load.wait()
    me = lax.axis_index("ocn")
    slots = packed_ref.shape[1]
    slot_rows = slots // 128
    slot_pad = -(-slot_rows // 8) * 8
    lines = col_ref.shape[0]
    lane = iota((1, 128), 1)

    offset = (dest_ref[...] - me) & (peers - 1)
    cells = cell_ref[...]
    classes = class_ref[...]
    cols = col_ref[...]
    area = jnp.zeros(cols.shape, f32)
    for i in range(area_ref.shape[0]):
        area = jnp.where(classes == i, area_ref[i], area)

    hits = [jnp.where(offset == k, 1.0, 0.0) for k in range(1, peers)]
    hot = jnp.concatenate(hits, axis=0)
    upper = jnp.where(iota((128, 128), 0) <= iota((128, 128), 1), 1.0, 0.0).astype(bf16)
    running = nn(hot.astype(bf16), upper)
    count = running.shape[0]
    totals = jnp.broadcast_to(running[:, 127:128], running.shape).astype(bf16)
    below = jnp.where(iota((count, count), 1) < iota((count, count), 0), 1.0, 0.0).astype(bf16)
    before = nn(below, totals)
    place_of = running + before - 1.0
    slot = jnp.full(cols.shape, -1.0, f32)
    for k in range(1, peers):
        at = (k - 1) * lines
        slot = jnp.where(offset == k, place_of[at : at + lines], slot)
    slot = slot.astype(i32)
    position = iota((slot_pad, 128), 0) * 128 + iota((slot_pad, 128), 1)
    segment = jnp.full((slot_pad, 128), 1, i32)
    for k in range(2, peers):
        at = (k - 1) * lines
        start = before[at : at + 1, :].astype(i32)
        segment = segment + jnp.where(position >= start, 1, 0)

    a1 = area.astype(bf16).astype(f32)
    a2 = (area - a1).astype(bf16).astype(f32)
    a3 = area - a1 - a2
    slot_f, cell_f = flat(slot), flat(cells)
    col_f = flat(cols)
    areas = [flat(a1), flat(a2), flat(a3)]
    col_low = (col_f & 255).astype(f32)
    col_high = lax.shift_right_arithmetic(col_f, 8).astype(f32)
    cell_low = cell_f & 127
    cell_high = lax.shift_right_arithmetic(cell_f, 7)
    got = place(
        lax.shift_right_arithmetic(slot_f, 7), slot_f & 127,
        [col_low, col_high] + areas + [cell_high.astype(f32), cell_low.astype(f32)], slot_pad,
    )
    keep = [flat(g[:slot_rows]) for g in got]
    s_low, s_high = keep[0].astype(i32), keep[1].astype(i32)
    s_area = keep[2] + keep[3] + keep[4]
    smap_ref[0:1, :] = s_low
    smap_ref[1:2, :] = s_high
    smap_ref[2:3, :] = flat(segment[:slot_rows])
    sarea_ref[...] = s_area

    local_high = jnp.where(flat(offset) == 0, cell_high, -1)
    own = place(local_high, cell_low, [col_low, col_high + 1.0] + areas, OY)
    o_low, o_high = own[0].astype(i32), own[1].astype(i32) - 1
    o_area = own[2] + own[3] + own[4]
    omap_ref[0:1, :] = flat(o_low)
    omap_ref[1:2, :] = flat(o_high)
    oarea_ref[...] = flat(o_area)

    blank = jnp.zeros((2, 128), f32)
    edge = []
    for m in (own[0], own[1], o_area):
        block = blank
        for b in range(4):
            part = m[b * 8 : (b + 1) * 8]
            for j in range(4):
                first = b * 32 + j * 8
                moved = roll(part, first + 4)
                pair = jnp.concatenate([moved[j : j + 1], moved[4 + j : 5 + j]], axis=0)
                block = jnp.where((lane >= first) & (lane < first + 8), pair, block)
        edge.append(flat(block))

    for load in loads[5:]:
        load.wait()
    fw_pad[...] = jnp.zeros_like(fw_pad)
    fw_pad[0:levels, :] = fw_ref[...]
    fw = fw_pad[...]
    pulled = []
    for v in range(NVAR):
        left = wide(doubled(wide(doubled(fw), flux_ref[:, v, :], nt)), inv_ref[:, v, :])
        pulled.append(doubled(left))

    for y in range(OY):
        at = pl.ds(y * OX, OX)
        t_ref[0:levels, at] = tracer_ref[pl.ds(y, levels, stride=OY), :]
        t_ref[levels : levels + 1, at] = land_ref[y : y + 1, :].astype(f32)
        t_ref[levels + 1 : width, at] = jnp.zeros((width - levels - 1, OX), f32)

    is_even = (lax.axis_index("atm") & 1) == 0
    top, bottom = t_ref[:, 0 : 4 * OX], t_ref[:, 28 * OX : 32 * OX]
    even_ref[...] = jnp.where(is_even, bottom, top).astype(bf16)
    odd_ref[...] = jnp.where(is_even, top, bottom).astype(bf16)

    for i in range(parts):
        state_loads[i].wait()
        for c in range(i * part_rows // NVAR, (i + 1) * part_rows // NVAR, 2):
            total = None
            for v in range(NVAR):
                term = wide(pulled[v], column_block(state_ref, v, c, 2))
                total = term if total is None else total + term
            at = slice(c * 128, (c + 2) * 128)
            forcing_ref[0, :, at], forcing_ref[1, :, at] = split(total)
    source = two_terms(forcing_ref)

    rows = gather(source, s_low, s_high, width) * s_area
    rows = pick(rows, keep[5:7], levels + 1).astype(bf16)
    packed_ref[...] = rows
    f_edge = gather(source, edge[0].astype(i32), edge[1].astype(i32) - 1, width) * edge[2]
    t_edge = border_block(t_ref[...], lane)
    lead = (lane & 7) < 4
    to_right, to_left = [], []
    for i in range(2):
        fe, te = row_of(f_edge, i), row_of(t_edge, i)
        to_right.append(jnp.where(lead, fe, roll(te, 4)))
        to_left.append(jnp.where(lead, roll(fe, -4), te))
    to_right = jnp.concatenate(to_right, axis=1)
    to_left = jnp.concatenate(to_left, axis=1)
    for mask, ref in zip(borders, side_refs):
        ref[:, 0:slots] = rows
        ref[:, slots : slots + 256] = jnp.where((me ^ mask) == me + 1, to_right, to_left).astype(
            bf16
        )


def local_kernel(width, forcing_ref, omap_ref, oarea_ref, out_ref):
    source = two_terms(forcing_ref)
    out_ref[...] = gather(source, omap_ref[0:1, :], omap_ref[1:2, :], width) * oarea_ref[...]


def receive_kernel(
    peers, levels, width, borders, early0, early1, packed_ref, smap_ref, local_ref, t_ref, *rest
):
    got = rest[: peers - 1]
    f_ref, fs_ref, ts_ref, cmap_ref, even_ref, odd_ref, edge_ref = rest[peers - 1 :]
    me = lax.axis_index("ocn")
    slots = packed_ref.shape[1]
    lane = iota((1, 128), 1)
    segment = smap_ref[2:3, :]
    chunks = slots // 256

    def meant_for(tile):
        total = jnp.zeros((width, slots), f32)
        for mask in range(peers):
            ref = packed_ref if mask == 0 else got[mask - 1]
            step = (tile - (me ^ mask)) & (peers - 1)
            total = jnp.where(segment == step, ref[:, 0:slots].astype(f32), total)
        high = total[levels + 1 : levels + 2, :].astype(i32)
        low = total[levels + 2 : levels + 3, :].astype(i32)
        return stacked(total.astype(bf16)), high, low

    index = iota((1, slots), 1)
    payload = [(index & 255).astype(f32), (lax.shift_right_arithmetic(index, 8) + 1).astype(f32)]

    source, high, low = meant_for(me)
    cell = high * 128 + low
    cmap_ref[0:1, :] = cell & 255
    cmap_ref[1:2, :] = lax.shift_right_arithmetic(cell, 8)
    where_low, where_high = place(high, low, payload, OY)
    f_ref[...] = local_ref[...] + gather(
        source, flat(where_low).astype(i32), flat(where_high).astype(i32) - 1, width
    )

    halo_f = None
    for step in (-1, 1):
        source, high, low = meant_for(me + step)
        at = low - 120 if step < 0 else low
        inside = (low >= 124) if step < 0 else (low < 4)
        block = lax.shift_right_arithmetic(high & 7, 2)
        spot = lax.shift_right_arithmetic(high, 3) * 32 + (high & 3) * 8 + at
        where_low, where_high = place(jnp.where(inside, block, -1), spot, payload, 8)
        part = gather(
            source, flat(where_low[:2]).astype(i32), flat(where_high[:2]).astype(i32) - 1, width
        )
        halo_f = part if halo_f is None else halo_f + part

    def side_from(tile):
        block = jnp.zeros((width, 256), f32)
        for mask in borders:
            block = jnp.where(
                (me ^ mask) == tile, got[mask - 1][:, slots : slots + 256].astype(f32), block
            )
        return block

    from_left, from_right = side_from(me - 1), side_from(me + 1)
    lead = (lane & 7) < 4
    side_f, side_t = [], []
    for i in range(2):
        fl, fr = row_of(from_left, i), row_of(from_right, i)
        side_f.append(jnp.where(lead, fr, roll(fl, 4)) + row_of(halo_f, i))
        side_t.append(jnp.where(lead, roll(fr, -4), fl))
    f_strips = strips(f_ref[...], jnp.concatenate(side_f, axis=1), lane)
    t_strips = strips(t_ref[...], jnp.concatenate(side_t, axis=1), lane)
    for j in range(STRIPS):
        fs_ref[:, j * OX : (j + 1) * OX] = f_strips[j]
        ts_ref[:, j * OX : (j + 1) * OX] = t_strips[j]

    def four(parts, first, source):
        block = jnp.zeros((width, OX), f32)
        for m in range(4):
            inside = (lane >= m * 32) & (lane < m * 32 + 32)
            block = jnp.where(inside, roll(parts[first + m], 32 * (m - source)), block)
        return block

    edges = [four(p, first, source) for p in (f_strips, t_strips)
             for first, source in ((0, 0), (4, 0), (0, 3), (4, 3))]
    edge_ref[...] = jnp.concatenate(edges, axis=1)
    top = jnp.concatenate([f_ref[:, 0 : 3 * OX], edges[0], edges[4]], axis=1)
    bottom = jnp.concatenate([f_ref[:, 29 * OX : 32 * OX], edges[3], edges[7]], axis=1)
    is_even = (lax.axis_index("atm") & 1) == 0
    even_ref[...] = jnp.where(is_even, bottom, top).astype(bf16)
    odd_ref[...] = jnp.where(is_even, top, bottom).astype(bf16)


def tile_row(ref, y):
    return ref[:, y * OX : (y + 1) * OX]


def not_there(lane):
    me, peers = lax.axis_index("ocn"), lax.axis_size("ocn")
    spot = lane & 31
    return ((me == 0) & (spot >= 12) & (spot < 16)) | (
        (me == peers - 1) & (spot >= 8) & (spot < 12)
    )


def fill_diffusivity(ref, dif_ref):
    width, levels = ref.shape[0], dif_ref.shape[1]
    diag = iota((width, levels), 0) == iota((width, levels), 1)
    column = jnp.sum(jnp.where(diag, dif_ref[...], 0.0), axis=1, keepdims=True)
    ref[...] = jnp.broadcast_to(column, ref.shape)


def count_rows(w8, n8, rows):
    for y in rows:
        here = tile_row(w8, y)
        n8[:, y * OX : (y + 1) * OX] = (
            tile_row(w8, y - 1) + tile_row(w8, y + 1) + roll(here, 1) + roll(here, -1)
        )


def substep_rows(rows, forcing, wet, counts, dif):
    for step in range(OSTEPS):
        new = list(rows)
        for y in range(step + 1, len(rows) - 1 - step):
            here = rows[y]
            lap = rows[y - 1] + rows[y + 1] + roll(here, 1) + roll(here, -1) - counts(y) * here
            new[y] = here + wet(y) * (dif * lap + forcing(y))
        rows = new
    return rows


def substep_strips(now, forcing, wet, counts, dif, ends):
    for step in range(OSTEPS):
        new = []
        for j, here in enumerate(now):
            up, down = ends(now, j)
            lap = up + down + roll(here, 1) + roll(here, -1) - counts[j] * here
            new.append(here + wet[j] * (dif * lap + forcing[j]))
        now = new
    return now


def merged(line, value, lane, b):
    value = jnp.where(lane < 4, roll(line, -(b * 32 + 16)), value)
    return jnp.where(lane >= 124, roll(line, 120 - b * 32), value)


def inner_kernel(
    levels, width, f_ref, fs_ref, t_ref, ts_ref, dif_ref, tt_ref, w8, n8, ws8, ns8, d8
):
    lane = iota((1, 128), 1)
    w8[...] = jnp.broadcast_to(t_ref[levels : levels + 1, :], w8.shape)
    count_rows(w8, n8, range(1, OY - 1))
    outside = not_there(lane)
    for j in range(STRIPS):
        line = tile_row(ts_ref, j)[levels : levels + 1, :]
        ws8[:, j * OX : (j + 1) * OX] = jnp.broadcast_to(jnp.where(outside, 0.0, line), (8, OX))

    def ends(parts, j):
        up = roll(parts[STRIPS - 1], 32) if j == 0 else parts[j - 1]
        down = roll(parts[0], 96) if j == STRIPS - 1 else parts[j + 1]
        return up, down

    parts = [tile_row(ws8, j) for j in range(STRIPS)]
    for j in range(STRIPS):
        up, down = ends(parts, j)
        ns8[:, j * OX : (j + 1) * OX] = up + down + roll(parts[j], 1) + roll(parts[j], -1)
    fill_diffusivity(d8, dif_ref)

    def group(g, carry):
        lev = pl.ds(pl.multiple_of(g * 8, 8), 8)
        dif = d8[lev, :]

        def load(ref, j):
            return ref[lev, j * OX : (j + 1) * OX]

        rows = substep_rows(
            [load(t_ref, y) * tile_row(w8, y) for y in range(OY)], lambda y: load(f_ref, y),
            lambda y: tile_row(w8, y), lambda y: tile_row(n8, y), dif,
        )
        wet = [tile_row(ws8, j) for j in range(STRIPS)]
        now = substep_strips(
            [load(ts_ref, j) * wet[j] for j in range(STRIPS)],
            [load(fs_ref, j) for j in range(STRIPS)], wet,
            [tile_row(ns8, j) for j in range(STRIPS)], dif, ends,
        )
        for y in range(4, OY - 4):
            value = merged(now[y % 8], rows[y], lane, y // 8)
            tt_ref[lev, y * OX : (y + 1) * OX] = jnp.where(
                tile_row(w8, y) > 0.0, value, load(t_ref, y)
            )
        return carry

    lax.fori_loop(0, width // 8, group, 0)


def slab_kernel(levels, t_ref, even_ref, odd_ref, s, w8, n8):
    row, rows_atm = lax.axis_index("atm"), lax.axis_size("atm")
    is_even = (row & 1) == 0
    even, odd = even_ref[...].astype(f32), odd_ref[...].astype(f32)
    top, bottom = jnp.where(is_even, odd, even), jnp.where(is_even, even, odd)
    tops = jnp.where(row > 0, 1.0, 0.0)
    bottoms = jnp.where(row < rows_atm - 1, 1.0, 0.0)

    def wide_wet(x):
        return jnp.broadcast_to(x[levels : levels + 1, :], (8, x.shape[1]))

    w8[:, 0 : 4 * OX] = wide_wet(top) * tops
    w8[:, 4 * OX : 12 * OX] = wide_wet(t_ref[:, 0 : 8 * OX])
    w8[:, 12 * OX : 20 * OX] = wide_wet(t_ref[:, 24 * OX : 32 * OX])
    w8[:, 20 * OX : 24 * OX] = wide_wet(bottom) * bottoms
    for y in (0, 11, 12, 23):
        n8[:, y * OX : (y + 1) * OX] = jnp.zeros((8, OX), f32)
    count_rows(w8, n8, list(range(1, 11)) + list(range(13, 23)))
    s[:, 0 : 4 * OX] = top * w8[0:1, 0 : 4 * OX]
    s[:, 4 * OX : 12 * OX] = t_ref[:, 0 : 8 * OX] * w8[0:1, 4 * OX : 12 * OX]
    s[:, 12 * OX : 20 * OX] = t_ref[:, 24 * OX : 32 * OX] * w8[0:1, 12 * OX : 20 * OX]
    s[:, 20 * OX : 24 * OX] = bottom * w8[0:1, 20 * OX : 24 * OX]


def outer_kernel(
    levels, width,
    f_ref, t_ref, edge_ref, inner_ref, even_ref, odd_ref, s, w8, n8, dif_ref, cmap_ref,
    tt_ref, back_ref,
    fx, se, we8, ne8, d8,
):
    row, rows_atm = lax.axis_index("atm"), lax.axis_size("atm")
    is_even = (row & 1) == 0
    lane = iota((1, 128), 1)
    block = lax.shift_right_arithmetic(lane, 5)
    even, odd = even_ref[...].astype(f32), odd_ref[...].astype(f32)
    top, bottom = jnp.where(is_even, odd, even), jnp.where(is_even, even, odd)
    tops = jnp.where(row > 0, 1.0, 0.0)
    bottoms = jnp.where(row < rows_atm - 1, 1.0, 0.0)

    def wide_wet(x):
        return jnp.broadcast_to(x[levels : levels + 1, :], (8, x.shape[1]))

    fx[:, OX : 4 * OX] = top[:, 0 : 3 * OX]
    fx[:, 4 * OX : 12 * OX] = f_ref[:, 0 : 8 * OX]
    fx[:, 12 * OX : 20 * OX] = f_ref[:, 24 * OX : 32 * OX]
    fx[:, 20 * OX : 23 * OX] = bottom[:, 0 : 3 * OX]
    outside = not_there(lane)
    for at, f_part, t_part, there in (
        (0, top[:, 384:512], top[:, 512:640], tops),
        (1, edge_ref[:, 0:128], edge_ref[:, 512:640], None),
        (2, edge_ref[:, 128:256], edge_ref[:, 640:768], None),
        (3, edge_ref[:, 256:384], edge_ref[:, 768:896], None),
        (4, edge_ref[:, 384:512], edge_ref[:, 896:1024], None),
        (5, bottom[:, 384:512], bottom[:, 512:640], bottoms),
    ):
        wet = jnp.where(outside, 0.0, wide_wet(t_part))
        wet = wet if there is None else wet * there
        we8[:, at * OX : (at + 1) * OX] = wet
        se[:, at * OX : (at + 1) * OX] = t_part * wet[0:1, :]
        se[:, (6 + at) * OX : (7 + at) * OX] = f_part

    def ends(parts, j):
        before = parts[j] if j % 3 == 0 else jnp.where(block == 3, parts[j - 1], parts[j])
        after = parts[j] if j % 3 == 2 else jnp.where(block == 0, parts[j + 1], parts[j])
        return roll(before, 32), roll(after, 96)

    parts = [tile_row(we8, j) for j in range(6)]
    for j in range(6):
        up, down = ends(parts, j)
        ne8[:, j * OX : (j + 1) * OX] = up + down + roll(parts[j], 1) + roll(parts[j], -1)
    fill_diffusivity(d8, dif_ref)
    tt_ref[:, 4 * OX : 28 * OX] = inner_ref[:, 4 * OX : 28 * OX]

    def group(g, carry):
        lev = pl.ds(pl.multiple_of(g * 8, 8), 8)
        dif = d8[lev, :]

        def load(ref, j):
            return ref[lev, j * OX : (j + 1) * OX]

        slabs = []
        for base in (0, 12):
            slabs += substep_rows(
                [load(s, base + y) for y in range(12)], lambda y: load(fx, base + y),
                lambda y: tile_row(w8, base + y), lambda y: tile_row(n8, base + y), dif,
            )
        now = substep_strips(
            [load(se, j) for j in range(6)], [load(se, 6 + j) for j in range(6)],
            [tile_row(we8, j) for j in range(6)], [tile_row(ne8, j) for j in range(6)], dif, ends,
        )
        for m in range(4):
            for y, slab, line in ((m, 4 + m, now[1]), (28 + m, 16 + m, now[4])):
                value = merged(line, slabs[slab], lane, m)
                tt_ref[lev, y * OX : (y + 1) * OX] = jnp.where(
                    tile_row(w8, slab) > 0.0, value, load(t_ref, y)
                )
        return carry

    lax.fori_loop(0, width // 8, group, 0)
    source = stacked(tt_ref[...].astype(bf16))
    back_ref[...] = gather(source, cmap_ref[0:1, :], cmap_ref[1:2, :], width).astype(bf16)


def state_kernel(levels, inv_ref, sw_ref, sm_ref, state_ref, out_ref, h_ref, sm_pad):
    sm_pad[...] = jnp.zeros_like(sm_pad)
    sm_pad[0:levels, :] = sm_ref[...]
    blocks = state_ref.shape[1] // NVAR
    for v in range(NVAR):
        inv = inv_ref[:, v, :]
        both = split(three(nn, inv, three(nt, sw_ref[:, v, :], sm_pad[...])))
        h_ref[v, 0], h_ref[v, 1] = both
        high, low = split(three(nn, inv, inv))
        for c in range(0, blocks, 2):
            sh, sl = split(column_block(state_ref, v, c, 2))
            out_ref[v, :, c * 128 : (c + 2) * 128] = nn(high, sh) + nn(high, sl) + nn(low, sh)


def sum_kernel(levels, width, tt_ref, omap_ref, oarea_ref, out_ref, tracer_ref):
    for y in range(OY):
        tracer_ref[pl.ds(y, levels, stride=OY), :] = tt_ref[0:levels, y * OX : (y + 1) * OX]
    count = out_ref.shape[1] // 256
    chunk = 1024
    total = None
    for start in range(0, OCELLS, chunk):
        at = slice(start, start + chunk)
        value = tt_ref[:, at] * oarea_ref[:, at]
        part = spread(value, omap_ref[0:1, at], omap_ref[1:2, at], count)
        total = part if total is None else total + part
    for h in range(count):
        out_ref[:, h * 256 : (h + 1) * 256] = total[h * width : (h + 1) * width]


def final_kernel(peers, width, smap_ref, sarea_ref, sum_ref, h_ref, base_ref, *rest):
    got = rest[: peers - 1]
    out_ref, sums = rest[peers - 1 :]
    step = pl.program_id(0)
    columns = sum_ref.shape[1]
    count = columns // 256

    @pl.when(step == 0)
    def _():
        me = lax.axis_index("ocn")
        segment = smap_ref[2:3, :]
        total = jnp.zeros((width, segment.shape[1]), f32)
        for mask in range(1, peers):
            offset = ((me ^ mask) - me) & (peers - 1)
            total = jnp.where(segment == offset, got[mask - 1][...].astype(f32), total)
        part = spread(total * sarea_ref[...], smap_ref[0:1, :], smap_ref[1:2, :], count)
        for h in range(count):
            at = slice(h * 256, (h + 1) * 256)
            sums[:, at] = part[h * width : (h + 1) * width] + sum_ref[:, at]

    size, rows, lanes = out_ref.shape
    lines = out_ref.reshape(size * rows, lanes)
    blocks = rows // NVAR
    first = pl.multiple_of(step * (blocks * 128), blocks * 128)
    sh, sl = split(sums[:, pl.ds(first, blocks * 128)])
    for v in range(NVAR):
        hh, hl = h_ref[v, 0], h_ref[v, 1]
        value = base_ref[v] + (nn(hh, sh) + nn(hh, sl) + nn(hl, sh))
        for c in range(blocks):
            lines[pl.ds(c * NVAR + v, size, stride=rows), :] = value[:, c * 128 : (c + 1) * 128]


def on_device(
    atmos_state, inverses, flux_weight, surface_weight, area_table, xc_column, xc_dest, xc_cell,
    xc_class, tracer, land_sea, forcing_weight, surface_map, diffusivity,
):
    peers, tiles = lax.axis_size("ocn"), lax.axis_size("atm")
    vars_, size, columns = atmos_state.shape
    cells = xc_column.shape[0]
    levels = tracer.shape[0]
    slots = cells - 3 * cells // peers
    width = -(-(levels + 3) // 16) * 16
    borders = sorted({i ^ (i + 1) for i in range(peers - 1)})
    sds = jax.ShapeDtypeStruct
    params = pltpu.CompilerParams(vmem_limit_bytes=30 * 1024 * 1024)
    vmem = pl.BlockSpec(memory_space=pltpu.VMEM)

    def swap(x, axis, pairs):
        return lax.ppermute(x, axis, pairs)

    def xor_swap(x, mask):
        return swap(x, "ocn", [(i, i ^ mask) for i in range(peers)])

    blocks = columns // 128
    by_level = lambda x: x.transpose(1, 0, 2)
    state = atmos_state.reshape(vars_, size, blocks, 128).transpose(1, 2, 0, 3)
    state = state.reshape(size, blocks * vars_, 128)
    inverse = by_level(inverses[0])
    hbm = pl.BlockSpec(memory_space=pltpu.HBM)
    anywhere = pl.BlockSpec(memory_space=pl.ANY)
    grid_of = lambda x: x.reshape(cells // 128, 128)
    small = [
        area_table, grid_of(xc_column), grid_of(xc_dest), grid_of(xc_cell), grid_of(xc_class),
        inverse, by_level(flux_weight), forcing_weight, tracer.reshape(levels * OY, OX), land_sea,
    ]
    outs = pl.pallas_call(
        functools.partial(send_kernel, peers, levels, width, borders),
        out_shape=[sds((width, slots), bf16)]
        + [sds((width, slots + 256), bf16)] * len(borders)
        + [sds((width, 4 * OX), bf16)] * 2
        + [
            sds((2, width, columns), bf16), sds((width, OCELLS), f32), sds((2, OCELLS), i32),
            sds((1, OCELLS), f32), sds((3, slots), i32), sds((1, slots), f32),
            sds(state.shape, f32),
        ],
        in_specs=[hbm] * 11,
        out_specs=[vmem] * (10 + len(borders)),
        scratch_shapes=[pltpu.SMEM(small[0].shape, f32)]
        + [pltpu.VMEM(x.shape, x.dtype) for x in small[1:]]
        + [
            pltpu.VMEM((width, forcing_weight.shape[1]), f32),
            pltpu.SemaphoreType.DMA((len(small),)), pltpu.SemaphoreType.DMA((4,)),
        ],
        compiler_params=params,
        name="send",
    )(*[pltpu.with_memory_space_constraint(x, pltpu.HBM) for x in small + [state]])
    packed, sides = outs[0], outs[1 : 1 + len(borders)]
    even_t, odd_t, forcing_cols, t0, omap, oarea, smap, sarea, state = outs[1 + len(borders) :]
    got = []
    for mask in range(1, peers):
        buffer = sides[borders.index(mask)] if mask in borders else packed
        got.append(xor_swap(buffer, mask))

    first = [(i, i ^ 1) for i in range(tiles)]
    second = [(i, (i + 1) % tiles if i & 1 else (i - 1) % tiles) for i in range(tiles)]
    even_t, odd_t = swap(even_t, "atm", first), swap(odd_t, "atm", second)

    local = pl.pallas_call(
        functools.partial(local_kernel, width),
        out_shape=sds((width, OCELLS), f32),
        in_specs=[vmem] * 3, out_specs=vmem, compiler_params=params, name="local",
    )(forcing_cols, omap, oarea)

    slab = 24 * OX
    slabs = pl.pallas_call(
        functools.partial(slab_kernel, levels),
        out_shape=[sds((width, slab), f32), sds((8, slab), f32), sds((8, slab), f32)],
        in_specs=[vmem] * 3, out_specs=[vmem] * 3, compiler_params=params, name="slab",
    )(t0, even_t, odd_t)

    base, back_map = pl.pallas_call(
        functools.partial(state_kernel, levels),
        out_shape=[sds((vars_, size, columns), f32), sds((vars_, 2, size, width), bf16)],
        in_specs=[vmem] * 4, out_specs=[vmem] * 2,
        scratch_shapes=[pltpu.VMEM((width, surface_map.shape[1]), f32)],
        compiler_params=params, name="state",
    )(inverse, by_level(surface_weight), surface_map, state)

    send_rows = 5 * OX
    f_all, fs, ts, cmap, even, odd, edge = pl.pallas_call(
        functools.partial(receive_kernel, peers, levels, width, borders),
        out_shape=[
            sds((width, OCELLS), f32), sds((width, STRIPS * OX), f32),
            sds((width, STRIPS * OX), f32), sds((2, slots), i32),
            sds((width, send_rows), bf16), sds((width, send_rows), bf16),
            sds((width, 8 * OX), f32),
        ],
        in_specs=[anywhere] * 2 + [vmem] * (3 + peers), out_specs=[vmem] * 7,
        compiler_params=params, name="receive",
    )(slabs[2], back_map, packed, smap, local, t0, *got)
    even, odd = swap(even, "atm", first), swap(odd, "atm", second)

    dif = diffusivity.reshape(1, levels)
    scratch = lambda *shapes: [pltpu.VMEM(shape, f32) for shape in shapes]
    inner = pl.pallas_call(
        functools.partial(inner_kernel, levels, width),
        out_shape=sds((width, OCELLS), f32),
        in_specs=[vmem] * 5, out_specs=vmem,
        scratch_shapes=scratch(
            (8, OCELLS), (8, OCELLS), (8, STRIPS * OX), (8, STRIPS * OX), (width, OX),
        ),
        compiler_params=params, name="inner",
    )(f_all, fs, t0, ts, dif)
    t4, back = pl.pallas_call(
        functools.partial(outer_kernel, levels, width),
        out_shape=[sds((width, OCELLS), f32), sds((width, slots), bf16)],
        in_specs=[vmem] * 11, out_specs=[vmem] * 2,
        scratch_shapes=scratch(
            (width, slab), (width, 12 * OX), (8, 6 * OX), (8, 6 * OX), (width, OX),
        ),
        compiler_params=params, name="outer",
    )(f_all, t0, edge, inner, even, odd, *slabs, dif, cmap)

    returned = [xor_swap(back, mask) for mask in range(1, peers)]
    sums, tracer_out = pl.pallas_call(
        functools.partial(sum_kernel, levels, width),
        out_shape=[sds((width, columns), f32), sds((levels * OY, OX), f32)],
        in_specs=[vmem] * 3, out_specs=[vmem] * 2, compiler_params=params, name="sum",
    )(t4, omap, oarea)

    block = 512
    final_state = pl.pallas_call(
        functools.partial(final_kernel, peers, width),
        out_shape=sds((size, blocks * vars_, 128), f32),
        grid=(columns // block,),
        in_specs=[
            pl.BlockSpec(smap.shape, lambda i: (0, 0)),
            pl.BlockSpec(sarea.shape, lambda i: (0, 0)),
            pl.BlockSpec((width, columns), lambda i: (0, 0)),
            pl.BlockSpec(back_map.shape, lambda i: (0, 0, 0, 0)),
            pl.BlockSpec((vars_, size, block), lambda i: (0, 0, i)),
        ]
        + [pl.BlockSpec((width, slots), lambda i: (0, 0))] * (peers - 1),
        out_specs=pl.BlockSpec((size, block // 128 * vars_, 128), lambda i: (0, i, 0)),
        scratch_shapes=[pltpu.VMEM((width, columns), f32)],
        compiler_params=params, name="final",
    )(smap, sarea, sums, back_map, base, *returned)
    final_state = final_state.reshape(size, blocks, vars_, 128).transpose(2, 0, 1, 3)
    final_state = final_state.reshape(vars_, size, columns)
    return (final_state, tracer_out.reshape(tracer.shape))


def solution(mesh):
    in_specs = (
        P(None, None, ("member", "atm", "ocn")),
        P("atm", None, None, None),
        P(),
        P(),
        P(),
        P(("atm", "ocn")),
        P(("atm", "ocn"), None),
        P(("atm", "ocn")),
        P(("atm", "ocn")),
        P(None, "atm", ("member", "ocn")),
        P("atm", "ocn"),
        P(),
        P(),
        P(),
    )
    out_specs = (P(None, None, ("member", "atm", "ocn")), P(None, "atm", ("member", "ocn")))
    return jax.shard_map(
        on_device, mesh=mesh, in_specs=in_specs, out_specs=out_specs, check_vma=False
    )
```

```python
import functools
import jax
import jax.numpy as jnp
from jax import lax
from jax.experimental import pallas as pl
from jax.experimental.pallas import tpu as pltpu
from jax.sharding import PartitionSpec as P

OSTEPS = 4
PAD = 8
NVAR = 4
OY = 32
OX = 128
OCELLS = OY * OX
STRIPS = 8
f32 = jnp.float32
bf16 = jnp.bfloat16
i32 = jnp.int32


def nn(a, b):
    return jnp.dot(a, b, preferred_element_type=f32)


def nt(a, b):
    return lax.dot_general(a, b, (((1,), (1,)), ((), ())), preferred_element_type=f32)


def split(x):
    high = x.astype(bf16)
    return high, (x - high.astype(f32)).astype(bf16)


def three(dot, a, b):
    ah, al = split(a)
    bh, bl = split(b)
    return dot(ah, bh) + dot(ah, bl) + dot(al, bh)


def doubled(x):
    return jnp.concatenate(list(split(x)), axis=0)


def wide(left, right, dot=nn):
    count = left.shape[0] // 2
    high, low = split(right)
    both = dot(left, high)
    return both[:count] + both[count:] + dot(left[:count], low)


def column_block(ref, var, first, blocks):
    size, rows, lanes = ref.shape
    lines = ref.reshape(size * rows, lanes)
    step = NVAR
    return jnp.concatenate(
        [lines[pl.ds((first + i) * step + var, size, stride=rows), :] for i in range(blocks)],
        axis=1,
    )


def iota(shape, dim):
    return lax.broadcasted_iota(i32, shape, dim)


def flat(x):
    return jnp.concatenate([x[i : i + 1, :] for i in range(x.shape[0])], axis=1)


def onehot(row, size):
    return jnp.where(iota((size, row.shape[1]), 0) == row, 1.0, 0.0).astype(bf16)


def place(high, low, payloads, rows):
    lines = iota((rows, high.shape[1]), 0) == high
    left = jnp.concatenate([jnp.where(lines, p, 0.0) for p in payloads], axis=0).astype(bf16)
    out = nt(left, onehot(low, 128))
    return [out[i * rows : (i + 1) * rows] for i in range(len(payloads))]


def stacked(x):
    return jnp.concatenate([x[:, h : h + 256] for h in range(0, x.shape[1], 256)], axis=0)


def two_terms(ref):
    return jnp.concatenate([stacked(ref[0]), stacked(ref[1])], axis=1)


def gather(source, low, high, width, chunk=512):
    count = source.shape[0] // width
    outs = []
    for start in range(0, low.shape[1], chunk):
        stop = min(start + chunk, low.shape[1])
        hot = onehot(low[:, start:stop], 256)
        if source.shape[1] == 512:
            hot = jnp.concatenate([hot, hot], axis=0)
        part = nn(source, hot)
        hc = high[:, start:stop]
        total = jnp.where(hc == 0, part[:width], 0.0)
        for h in range(1, count):
            total = jnp.where(hc == h, part[h * width : (h + 1) * width], total)
        outs.append(total)
    return outs[0] if len(outs) == 1 else jnp.concatenate(outs, axis=1)


def spread(value, low, high, count):
    vh, vl = split(value)
    hot = onehot(low, 256)
    outs = []
    for term in (vh, vl):
        parts = [jnp.where(high == h, term.astype(f32), 0.0) for h in range(count)]
        outs.append(nt(jnp.concatenate(parts, axis=0).astype(bf16), hot))
    return outs[0] + outs[1]


def pick(level_rows, lane_rows, base):
    index = iota(level_rows.shape, 0)
    for i, row in enumerate(lane_rows):
        level_rows = jnp.where(index == base + i, row, level_rows)
    return level_rows


def roll(x, shift):
    shift = shift % 128
    return x if shift == 0 else pltpu.roll(x, shift, 1)


def row_of(x, y):
    return x[:, y * OX : (y + 1) * OX]


def border_block(x, lane):
    blocks = []
    for i in range(2):
        block = jnp.zeros((x.shape[0], OX), f32)
        for b in range(4):
            for j in range(4):
                first = b * 32 + j * 8
                moved = roll(row_of(x, b * 8 + i * 4 + j), first + 4)
                block = jnp.where((lane >= first) & (lane < first + 8), moved, block)
        blocks.append(block)
    return jnp.concatenate(blocks, axis=1)


def strips(x, halo, lane):
    outs = []
    for j in range(STRIPS):
        side = roll(row_of(halo, j // 4), 8 - (j % 4) * 8)
        for b in range(4):
            line = row_of(x, b * 8 + j)
            first = b * 32
            side = jnp.where((lane >= first) & (lane < first + 8), roll(line, first + 8), side)
            side = jnp.where(
                (lane >= first + 16) & (lane < first + 24), roll(line, first + 16), side
            )
        outs.append(side)
    return outs


def send_kernel(
    peers, levels, width, borders,
    *refs,
):
    sources, rest = refs[:11], refs[11:]
    packed_ref, rest = rest[0], rest[1:]
    side_refs, rest = rest[: len(borders)], rest[len(borders) :]
    (even_ref, odd_ref), rest = rest[:2], rest[2:]
    forcing_ref, t_ref, omap_ref, oarea_ref, smap_ref, sarea_ref, state_ref = rest[:7]
    staged, fw_pad, sems, state_sems = rest[7:17], rest[17], rest[18], rest[19]
    (area_ref, col_ref, dest_ref, cell_ref, class_ref, inv_ref, flux_ref, fw_ref, tracer_ref,
     land_ref) = staged
    loads = [
        pltpu.make_async_copy(a, b.at[:, pl.ds(0, OY), :] if b is tracer_ref else b, sems.at[i])
        for i, (a, b) in enumerate(zip(sources[:10], staged))
    ]
    for load in loads:
        load.start()
    state_hbm = sources[10]
    parts = state_sems.shape[0]
    part_rows = state_hbm.shape[1] // parts
    state_loads = []
    for i in range(parts):
        at = pl.ds(i * part_rows, part_rows)
        state_loads.append(
            pltpu.make_async_copy(
                state_hbm.at[:, at, :], state_ref.at[:, at, :], state_sems.at[i]
            )
        )
        state_loads[i].start()
    for load in loads[:5]:
        load.wait()
    me = lax.axis_index("ocn")
    slots = packed_ref.shape[1]
    slot_rows = slots // 128
    slot_pad = -(-slot_rows // 8) * 8
    lines = col_ref.shape[0]
    lane = iota((1, 128), 1)

    offset = (dest_ref[...] - me) & (peers - 1)
    cells = cell_ref[...]
    classes = class_ref[...]
    cols = col_ref[...]
    area = jnp.zeros(cols.shape, f32)
    for i in range(area_ref.shape[0]):
        area = jnp.where(classes == i, area_ref[i], area)

    hits = [jnp.where(offset == k, 1.0, 0.0) for k in range(1, peers)]
    hot = jnp.concatenate(hits, axis=0)
    upper = jnp.where(iota((128, 128), 0) <= iota((128, 128), 1), 1.0, 0.0).astype(bf16)
    running = nn(hot.astype(bf16), upper)
    count = running.shape[0]
    totals = jnp.broadcast_to(running[:, 127:128], running.shape).astype(bf16)
    below = jnp.where(iota((count, count), 1) < iota((count, count), 0), 1.0, 0.0).astype(bf16)
    before = nn(below, totals)
    place_of = running + before - 1.0
    slot = jnp.full(cols.shape, -1.0, f32)
    for k in range(1, peers):
        at = (k - 1) * lines
        slot = jnp.where(offset == k, place_of[at : at + lines], slot)
    slot = slot.astype(i32)
    position = iota((slot_pad, 128), 0) * 128 + iota((slot_pad, 128), 1)
    segment = jnp.full((slot_pad, 128), 1, i32)
    for k in range(2, peers):
        at = (k - 1) * lines
        start = before[at : at + 1, :].astype(i32)
        segment = segment + jnp.where(position >= start, 1, 0)

    a1 = area.astype(bf16).astype(f32)
    a2 = (area - a1).astype(bf16).astype(f32)
    a3 = area - a1 - a2
    slot_f, cell_f = flat(slot), flat(cells)
    col_f = flat(cols)
    areas = [flat(a1), flat(a2), flat(a3)]
    col_low = (col_f & 255).astype(f32)
    col_high = lax.shift_right_arithmetic(col_f, 8).astype(f32)
    cell_low = cell_f & 127
    cell_high = lax.shift_right_arithmetic(cell_f, 7)
    got = place(
        lax.shift_right_arithmetic(slot_f, 7), slot_f & 127,
        [col_low, col_high] + areas + [cell_high.astype(f32), cell_low.astype(f32)], slot_pad,
    )
    keep = [flat(g[:slot_rows]) for g in got]
    s_low, s_high = keep[0].astype(i32), keep[1].astype(i32)
    s_area = keep[2] + keep[3] + keep[4]
    smap_ref[0:1, :] = s_low
    smap_ref[1:2, :] = s_high
    smap_ref[2:3, :] = flat(segment[:slot_rows])
    sarea_ref[...] = s_area

    local_high = jnp.where(flat(offset) == 0, cell_high, -1)
    own = place(local_high, cell_low, [col_low, col_high + 1.0] + areas, OY)
    o_low, o_high = own[0].astype(i32), own[1].astype(i32) - 1
    o_area = own[2] + own[3] + own[4]
    omap_ref[0:1, :] = flat(o_low)
    omap_ref[1:2, :] = flat(o_high)
    oarea_ref[...] = flat(o_area)

    blank = jnp.zeros((2, 128), f32)
    edge = []
    for m in (own[0], own[1], o_area):
        block = blank
        for b in range(4):
            part = m[b * 8 : (b + 1) * 8]
            for j in range(4):
                first = b * 32 + j * 8
                moved = roll(part, first + 4)
                pair = jnp.concatenate([moved[j : j + 1], moved[4 + j : 5 + j]], axis=0)
                block = jnp.where((lane >= first) & (lane < first + 8), pair, block)
        edge.append(flat(block))

    for load in loads[5:]:
        load.wait()
    fw_pad[...] = jnp.zeros_like(fw_pad)
    fw_pad[0:levels, :] = fw_ref[...]
    fw = fw_pad[...]
    size = inv_ref.shape[0]
    flux = flux_ref[...].reshape(size * NVAR, flux_ref.shape[2])
    mixed = wide(doubled(fw), flux, nt)
    which = iota((1, size * NVAR), 1) & (NVAR - 1)
    masked = jnp.concatenate([jnp.where(which == v, mixed, 0.0) for v in range(NVAR)], axis=0)
    drawn = wide(doubled(masked), inv_ref[...].reshape(size * NVAR, size))
    pulled = [doubled(drawn[v * width : (v + 1) * width]) for v in range(NVAR)]

    tracer_lines = tracer_ref.reshape(levels * (OY + PAD), OX)
    for y in range(OY):
        at = pl.ds(y * OX, OX)
        t_ref[0:levels, at] = tracer_lines[pl.ds(y, levels, stride=OY + PAD), :]
        t_ref[levels : levels + 1, at] = land_ref[y : y + 1, :].astype(f32)
        t_ref[levels + 1 : width, at] = jnp.zeros((width - levels - 1, OX), f32)

    is_even = (lax.axis_index("atm") & 1) == 0
    top, bottom = t_ref[:, 0 : 4 * OX], t_ref[:, 28 * OX : 32 * OX]
    even_ref[...] = jnp.where(is_even, bottom, top).astype(bf16)
    odd_ref[...] = jnp.where(is_even, top, bottom).astype(bf16)

    for i in range(parts):
        state_loads[i].wait()
        for c in range(i * part_rows // NVAR, (i + 1) * part_rows // NVAR, 2):
            total = None
            for v in range(NVAR):
                term = wide(pulled[v], column_block(state_ref, v, c, 2))
                total = term if total is None else total + term
            at = slice(c * 128, (c + 2) * 128)
            forcing_ref[0, :, at], forcing_ref[1, :, at] = split(total)
    source = two_terms(forcing_ref)

    rows = gather(source, s_low, s_high, width) * s_area
    rows = pick(rows, keep[5:7], levels + 1).astype(bf16)
    packed_ref[...] = rows
    f_edge = gather(source, edge[0].astype(i32), edge[1].astype(i32) - 1, width) * edge[2]
    t_edge = border_block(t_ref[...], lane)
    lead = (lane & 7) < 4
    to_right, to_left = [], []
    for i in range(2):
        fe, te = row_of(f_edge, i), row_of(t_edge, i)
        to_right.append(jnp.where(lead, fe, roll(te, 4)))
        to_left.append(jnp.where(lead, roll(fe, -4), te))
    to_right = jnp.concatenate(to_right, axis=1)
    to_left = jnp.concatenate(to_left, axis=1)
    for mask, ref in zip(borders, side_refs):
        ref[:, 0:slots] = rows
        ref[:, slots : slots + 256] = jnp.where((me ^ mask) == me + 1, to_right, to_left).astype(
            bf16
        )


def local_kernel(width, forcing_ref, omap_ref, oarea_ref, out_ref):
    source = two_terms(forcing_ref)
    out_ref[...] = gather(source, omap_ref[0:1, :], omap_ref[1:2, :], width) * oarea_ref[...]


def receive_kernel(
    peers, levels, width, borders, early0, early1, packed_ref, smap_ref, local_ref, t_ref, *rest
):
    got = rest[: peers - 1]
    f_ref, fs_ref, ts_ref, cmap_ref, even_ref, odd_ref, edge_ref = rest[peers - 1 :]
    me = lax.axis_index("ocn")
    slots = packed_ref.shape[1]
    lane = iota((1, 128), 1)
    segment = smap_ref[2:3, :]
    chunks = slots // 256

    def meant_for(tile):
        total = jnp.zeros((width, slots), f32)
        for mask in range(peers):
            ref = packed_ref if mask == 0 else got[mask - 1]
            step = (tile - (me ^ mask)) & (peers - 1)
            total = jnp.where(segment == step, ref[:, 0:slots].astype(f32), total)
        high = total[levels + 1 : levels + 2, :].astype(i32)
        low = total[levels + 2 : levels + 3, :].astype(i32)
        return stacked(total.astype(bf16)), high, low

    index = iota((1, slots), 1)
    payload = [(index & 255).astype(f32), (lax.shift_right_arithmetic(index, 8) + 1).astype(f32)]

    source, high, low = meant_for(me)
    cell = high * 128 + low
    cmap_ref[0:1, :] = cell & 255
    cmap_ref[1:2, :] = lax.shift_right_arithmetic(cell, 8)
    where_low, where_high = place(high, low, payload, OY)
    f_ref[...] = local_ref[...] + gather(
        source, flat(where_low).astype(i32), flat(where_high).astype(i32) - 1, width
    )

    halo_f = None
    for step in (-1, 1):
        source, high, low = meant_for(me + step)
        at = low - 120 if step < 0 else low
        inside = (low >= 124) if step < 0 else (low < 4)
        block = lax.shift_right_arithmetic(high & 7, 2)
        spot = lax.shift_right_arithmetic(high, 3) * 32 + (high & 3) * 8 + at
        where_low, where_high = place(jnp.where(inside, block, -1), spot, payload, 8)
        part = gather(
            source, flat(where_low[:2]).astype(i32), flat(where_high[:2]).astype(i32) - 1, width
        )
        halo_f = part if halo_f is None else halo_f + part

    def side_from(tile):
        block = jnp.zeros((width, 256), f32)
        for mask in borders:
            block = jnp.where(
                (me ^ mask) == tile, got[mask - 1][:, slots : slots + 256].astype(f32), block
            )
        return block

    from_left, from_right = side_from(me - 1), side_from(me + 1)
    lead = (lane & 7) < 4
    side_f, side_t = [], []
    for i in range(2):
        fl, fr = row_of(from_left, i), row_of(from_right, i)
        side_f.append(jnp.where(lead, fr, roll(fl, 4)) + row_of(halo_f, i))
        side_t.append(jnp.where(lead, roll(fr, -4), fl))
    f_strips = strips(f_ref[...], jnp.concatenate(side_f, axis=1), lane)
    t_strips = strips(t_ref[...], jnp.concatenate(side_t, axis=1), lane)
    for j in range(STRIPS):
        fs_ref[:, j * OX : (j + 1) * OX] = f_strips[j]
        ts_ref[:, j * OX : (j + 1) * OX] = t_strips[j]

    def four(parts, first, source):
        block = jnp.zeros((width, OX), f32)
        for m in range(4):
            inside = (lane >= m * 32) & (lane < m * 32 + 32)
            block = jnp.where(inside, roll(parts[first + m], 32 * (m - source)), block)
        return block

    edges = [four(p, first, source) for p in (f_strips, t_strips)
             for first, source in ((0, 0), (4, 0), (0, 3), (4, 3))]
    edge_ref[...] = jnp.concatenate(edges, axis=1)
    top = jnp.concatenate([f_ref[:, 0 : 3 * OX], edges[0], edges[4]], axis=1)
    bottom = jnp.concatenate([f_ref[:, 29 * OX : 32 * OX], edges[3], edges[7]], axis=1)
    is_even = (lax.axis_index("atm") & 1) == 0
    even_ref[...] = jnp.where(is_even, bottom, top).astype(bf16)
    odd_ref[...] = jnp.where(is_even, top, bottom).astype(bf16)


def tile_row(ref, y):
    return ref[:, y * OX : (y + 1) * OX]


def not_there(lane):
    me, peers = lax.axis_index("ocn"), lax.axis_size("ocn")
    spot = lane & 31
    return ((me == 0) & (spot >= 12) & (spot < 16)) | (
        (me == peers - 1) & (spot >= 8) & (spot < 12)
    )


def fill_diffusivity(ref, dif_ref):
    width, levels = ref.shape[0], dif_ref.shape[1]
    diag = iota((width, levels), 0) == iota((width, levels), 1)
    column = jnp.sum(jnp.where(diag, dif_ref[...], 0.0), axis=1, keepdims=True)
    ref[...] = jnp.broadcast_to(column, ref.shape)


def count_rows(w8, n8, rows):
    for y in rows:
        here = tile_row(w8, y)
        n8[:, y * OX : (y + 1) * OX] = (
            tile_row(w8, y - 1) + tile_row(w8, y + 1) + roll(here, 1) + roll(here, -1)
        )


def substep_rows(rows, forcing, wet, counts, dif):
    for step in range(OSTEPS):
        new = list(rows)
        for y in range(step + 1, len(rows) - 1 - step):
            here = rows[y]
            lap = rows[y - 1] + rows[y + 1] + roll(here, 1) + roll(here, -1) - counts(y) * here
            new[y] = here + wet(y) * (dif * lap + forcing(y))
        rows = new
    return rows


def substep_strips(now, forcing, wet, counts, dif, ends):
    for step in range(OSTEPS):
        new = []
        for j, here in enumerate(now):
            up, down = ends(now, j)
            lap = up + down + roll(here, 1) + roll(here, -1) - counts[j] * here
            new.append(here + wet[j] * (dif * lap + forcing[j]))
        now = new
    return now


def tall(ref, j, count):
    return jnp.concatenate([tile_row(ref, j)] * (count // 8), axis=0)


def merged(line, value, lane, b):
    value = jnp.where(lane < 4, roll(line, -(b * 32 + 16)), value)
    return jnp.where(lane >= 124, roll(line, 120 - b * 32), value)


def inner_kernel(
    levels, width, f_ref, fs_ref, t_ref, ts_ref, dif_ref, tt_ref, strip, w8, n8, ws8, ns8, d8
):
    lane = iota((1, 128), 1)
    w8[...] = jnp.broadcast_to(t_ref[levels : levels + 1, :], w8.shape)
    count_rows(w8, n8, range(1, OY - 1))
    outside = not_there(lane)
    for j in range(STRIPS):
        line = tile_row(ts_ref, j)[levels : levels + 1, :]
        ws8[:, j * OX : (j + 1) * OX] = jnp.broadcast_to(jnp.where(outside, 0.0, line), (8, OX))

    def ends(parts, j):
        up = roll(parts[STRIPS - 1], 32) if j == 0 else parts[j - 1]
        down = roll(parts[0], 96) if j == STRIPS - 1 else parts[j + 1]
        return up, down

    parts = [tile_row(ws8, j) for j in range(STRIPS)]
    for j in range(STRIPS):
        up, down = ends(parts, j)
        ns8[:, j * OX : (j + 1) * OX] = up + down + roll(parts[j], 1) + roll(parts[j], -1)
    fill_diffusivity(d8, dif_ref)

    half = width // 2

    def strip_group(g, carry):
        lev = pl.ds(pl.multiple_of(g * half, 8), half)

        def load(ref, j):
            return ref[lev, j * OX : (j + 1) * OX]

        wet = [tall(ws8, j, half) for j in range(STRIPS)]
        now = substep_strips(
            [load(ts_ref, j) * wet[j] for j in range(STRIPS)],
            [load(fs_ref, j) for j in range(STRIPS)], wet,
            [tall(ns8, j, half) for j in range(STRIPS)], d8[lev, :], ends,
        )
        for j in range(STRIPS):
            strip[lev, j * OX : (j + 1) * OX] = now[j]
        return carry

    lax.fori_loop(0, 2, strip_group, 0)

    def group(g, carry):
        lev = pl.ds(pl.multiple_of(g * 8, 8), 8)
        dif = d8[lev, :]

        def load(ref, j):
            return ref[lev, j * OX : (j + 1) * OX]

        rows = substep_rows(
            [load(t_ref, y) * tile_row(w8, y) for y in range(OY)], lambda y: load(f_ref, y),
            lambda y: tile_row(w8, y), lambda y: tile_row(n8, y), dif,
        )
        now = [load(strip, j) for j in range(STRIPS)]
        for y in range(4, OY - 4):
            value = merged(now[y % 8], rows[y], lane, y // 8)
            tt_ref[lev, y * OX : (y + 1) * OX] = jnp.where(
                tile_row(w8, y) > 0.0, value, load(t_ref, y)
            )
        return carry

    lax.fori_loop(0, width // 8, group, 0)


def slab_kernel(levels, t_ref, even_ref, odd_ref, s, w8, n8):
    row, rows_atm = lax.axis_index("atm"), lax.axis_size("atm")
    is_even = (row & 1) == 0
    even, odd = even_ref[...].astype(f32), odd_ref[...].astype(f32)
    top, bottom = jnp.where(is_even, odd, even), jnp.where(is_even, even, odd)
    tops = jnp.where(row > 0, 1.0, 0.0)
    bottoms = jnp.where(row < rows_atm - 1, 1.0, 0.0)

    def wide_wet(x):
        return jnp.broadcast_to(x[levels : levels + 1, :], (8, x.shape[1]))

    w8[:, 0 : 4 * OX] = wide_wet(top) * tops
    w8[:, 4 * OX : 12 * OX] = wide_wet(t_ref[:, 0 : 8 * OX])
    w8[:, 12 * OX : 20 * OX] = wide_wet(t_ref[:, 24 * OX : 32 * OX])
    w8[:, 20 * OX : 24 * OX] = wide_wet(bottom) * bottoms
    for y in (0, 11, 12, 23):
        n8[:, y * OX : (y + 1) * OX] = jnp.zeros((8, OX), f32)
    count_rows(w8, n8, list(range(1, 11)) + list(range(13, 23)))
    s[:, 0 : 4 * OX] = top * w8[0:1, 0 : 4 * OX]
    s[:, 4 * OX : 12 * OX] = t_ref[:, 0 : 8 * OX] * w8[0:1, 4 * OX : 12 * OX]
    s[:, 12 * OX : 20 * OX] = t_ref[:, 24 * OX : 32 * OX] * w8[0:1, 12 * OX : 20 * OX]
    s[:, 20 * OX : 24 * OX] = bottom * w8[0:1, 20 * OX : 24 * OX]


def outer_kernel(
    levels, width,
    f_ref, t_ref, edge_ref, inner_ref, even_ref, odd_ref, s, w8, n8, dif_ref, cmap_ref,
    tt_ref, back_ref,
    fx, se, we8, ne8, d8,
):
    row, rows_atm = lax.axis_index("atm"), lax.axis_size("atm")
    is_even = (row & 1) == 0
    lane = iota((1, 128), 1)
    block = lax.shift_right_arithmetic(lane, 5)
    even, odd = even_ref[...].astype(f32), odd_ref[...].astype(f32)
    top, bottom = jnp.where(is_even, odd, even), jnp.where(is_even, even, odd)
    tops = jnp.where(row > 0, 1.0, 0.0)
    bottoms = jnp.where(row < rows_atm - 1, 1.0, 0.0)

    def wide_wet(x):
        return jnp.broadcast_to(x[levels : levels + 1, :], (8, x.shape[1]))

    fx[:, OX : 4 * OX] = top[:, 0 : 3 * OX]
    fx[:, 4 * OX : 12 * OX] = f_ref[:, 0 : 8 * OX]
    fx[:, 12 * OX : 20 * OX] = f_ref[:, 24 * OX : 32 * OX]
    fx[:, 20 * OX : 23 * OX] = bottom[:, 0 : 3 * OX]
    outside = not_there(lane)
    for at, f_part, t_part, there in (
        (0, top[:, 384:512], top[:, 512:640], tops),
        (1, edge_ref[:, 0:128], edge_ref[:, 512:640], None),
        (2, edge_ref[:, 128:256], edge_ref[:, 640:768], None),
        (3, edge_ref[:, 256:384], edge_ref[:, 768:896], None),
        (4, edge_ref[:, 384:512], edge_ref[:, 896:1024], None),
        (5, bottom[:, 384:512], bottom[:, 512:640], bottoms),
    ):
        wet = jnp.where(outside, 0.0, wide_wet(t_part))
        wet = wet if there is None else wet * there
        we8[:, at * OX : (at + 1) * OX] = wet
        se[:, at * OX : (at + 1) * OX] = t_part * wet[0:1, :]
        se[:, (6 + at) * OX : (7 + at) * OX] = f_part

    def ends(parts, j):
        before = parts[j] if j % 3 == 0 else jnp.where(block == 3, parts[j - 1], parts[j])
        after = parts[j] if j % 3 == 2 else jnp.where(block == 0, parts[j + 1], parts[j])
        return roll(before, 32), roll(after, 96)

    parts = [tile_row(we8, j) for j in range(6)]
    for j in range(6):
        up, down = ends(parts, j)
        ne8[:, j * OX : (j + 1) * OX] = up + down + roll(parts[j], 1) + roll(parts[j], -1)
    fill_diffusivity(d8, dif_ref)
    tt_ref[:, 4 * OX : 28 * OX] = inner_ref[:, 4 * OX : 28 * OX]

    half = width // 2

    def strip_group(g, carry):
        lev = pl.ds(pl.multiple_of(g * half, 8), half)

        def load(ref, j):
            return ref[lev, j * OX : (j + 1) * OX]

        now = substep_strips(
            [load(se, j) for j in range(6)], [load(se, 6 + j) for j in range(6)],
            [tall(we8, j, half) for j in range(6)], [tall(ne8, j, half) for j in range(6)],
            d8[lev, :], ends,
        )
        se[lev, 0:OX], se[lev, OX : 2 * OX] = now[1], now[4]
        return carry

    lax.fori_loop(0, 2, strip_group, 0)

    def group(g, carry):
        lev = pl.ds(pl.multiple_of(g * 16, 16), 16)
        dif = d8[lev, :]

        def load(ref, j):
            return ref[lev, j * OX : (j + 1) * OX]

        slabs = []
        for base in (0, 12):
            slabs += substep_rows(
                [load(s, base + y) for y in range(12)], lambda y: load(fx, base + y),
                lambda y: tall(w8, base + y, 16), lambda y: tall(n8, base + y, 16), dif,
            )
        for m in range(4):
            for y, slab, line in ((m, 4 + m, load(se, 0)), (28 + m, 16 + m, load(se, 1))):
                value = merged(line, slabs[slab], lane, m)
                tt_ref[lev, y * OX : (y + 1) * OX] = jnp.where(
                    tall(w8, slab, 16) > 0.0, value, load(t_ref, y)
                )
        return carry

    lax.fori_loop(0, width // 16, group, 0)
    source = stacked(tt_ref[...].astype(bf16))
    back_ref[...] = gather(source, cmap_ref[0:1, :], cmap_ref[1:2, :], width).astype(bf16)


def state_kernel(levels, inv_ref, sw_ref, sm_ref, state_ref, out_ref, h_ref, sm_pad, square):
    sm_pad[...] = jnp.zeros_like(sm_pad)
    sm_pad[0:levels, :] = sm_ref[...]
    h_ref[...] = jnp.zeros_like(h_ref)
    square[...] = jnp.zeros_like(square)
    blocks = (state_ref.shape[1] - PAD) // NVAR
    size = inv_ref.shape[0]
    room = h_ref.shape[0] // (2 * NVAR)
    for v in range(NVAR):
        inv = inv_ref[:, v, :]
        high, low = split(three(nn, inv, three(nt, sw_ref[:, v, :], sm_pad[...])))
        h_ref[v * room : v * room + size, :] = high
        h_ref[(NVAR + v) * room : (NVAR + v) * room + size, :] = low
        square[v, 0:size, :], square[v, room : room + size, :] = split(three(nn, inv, inv))
    for v in range(NVAR):
        for c in range(0, blocks, 2):
            value = wide(square[v], column_block(state_ref, v, c, 2))
            out_ref[v, :, c * 128 : (c + 2) * 128] = value[:size]


def sum_kernel(levels, width, tt_ref, omap_ref, oarea_ref, out_ref, tracer_hbm, rows, sem):
    lines = rows.reshape(levels * (OY + PAD), OX)
    for y in range(OY):
        lines[pl.ds(y, levels, stride=OY + PAD), :] = tt_ref[0:levels, y * OX : (y + 1) * OX]
    store = pltpu.make_async_copy(rows.at[:, pl.ds(0, OY), :], tracer_hbm, sem)
    store.start()
    count = out_ref.shape[1] // 256
    chunk = 1024
    total = None
    for start in range(0, OCELLS, chunk):
        at = slice(start, start + chunk)
        value = tt_ref[:, at] * oarea_ref[:, at]
        part = spread(value, omap_ref[0:1, at], omap_ref[1:2, at], count)
        total = part if total is None else total + part
    for h in range(count):
        out_ref[:, h * 256 : (h + 1) * 256] = total[h * width : (h + 1) * width]
    store.wait()


def final_kernel(peers, width, smap_ref, sarea_ref, sum_ref, h_ref, base_ref, *rest):
    got = rest[: peers - 1]
    out_hbm, rows, sums, sems = rest[peers - 1 :]
    columns = sum_ref.shape[1]
    count = columns // 256
    me = lax.axis_index("ocn")
    segment = smap_ref[2:3, :]
    total = jnp.zeros((width, segment.shape[1]), f32)
    for mask in range(1, peers):
        offset = ((me ^ mask) - me) & (peers - 1)
        total = jnp.where(segment == offset, got[mask - 1][...].astype(f32), total)
    part = spread(total * sarea_ref[...], smap_ref[0:1, :], smap_ref[1:2, :], count)
    for h in range(count):
        at = slice(h * 256, (h + 1) * 256)
        sums[:, at] = part[h * width : (h + 1) * width] + sum_ref[:, at]

    size, stride, lanes = rows.shape
    lines = rows.reshape(size * stride, lanes)
    parts = sems.shape[0]
    room = h_ref.shape[0] // (2 * NVAR)
    stores = []
    for i in range(parts):
        share = columns // parts
        for c in range(i * share, (i + 1) * share, 256):
            every = wide(h_ref[...], sums[:, c : c + 256])
            for v in range(NVAR):
                value = base_ref[v, :, c : c + 256] + every[v * room : v * room + size]
                for k in range(2):
                    first = (c // 128 + k) * NVAR + v
                    lines[pl.ds(first, size, stride=stride), :] = value[:, k * 128 : k * 128 + 128]
        at = pl.ds(i * (share // 128 * NVAR), share // 128 * NVAR)
        store = pltpu.make_async_copy(rows.at[:, at, :], out_hbm.at[:, at, :], sems.at[i])
        store.start()
        stores.append(store)
    for store in stores:
        store.wait()


def on_device(
    atmos_state, inverses, flux_weight, surface_weight, area_table, xc_column, xc_dest, xc_cell,
    xc_class, tracer, land_sea, forcing_weight, surface_map, diffusivity,
):
    peers, tiles = lax.axis_size("ocn"), lax.axis_size("atm")
    vars_, size, columns = atmos_state.shape
    cells = xc_column.shape[0]
    levels = tracer.shape[0]
    slots = cells - 3 * cells // peers
    width = -(-(levels + 3) // 16) * 16
    borders = sorted({i ^ (i + 1) for i in range(peers - 1)})
    sds = jax.ShapeDtypeStruct
    params = pltpu.CompilerParams(vmem_limit_bytes=30 * 1024 * 1024)
    vmem = pl.BlockSpec(memory_space=pltpu.VMEM)

    def swap(x, axis, pairs):
        return lax.ppermute(x, axis, pairs)

    def xor_swap(x, mask):
        return swap(x, "ocn", [(i, i ^ mask) for i in range(peers)])

    blocks = columns // 128
    room = -(-size // 16) * 16
    by_level = lambda x: x.transpose(1, 0, 2)
    state = atmos_state.reshape(vars_, size, blocks, 128).transpose(1, 2, 0, 3)
    state = state.reshape(size, blocks * vars_, 128)
    inverse = by_level(inverses[0])
    hbm = pl.BlockSpec(memory_space=pltpu.HBM)
    anywhere = pl.BlockSpec(memory_space=pl.ANY)
    grid_of = lambda x: x.reshape(cells // 128, 128)
    small = [
        area_table, grid_of(xc_column), grid_of(xc_dest), grid_of(xc_cell), grid_of(xc_class),
        inverse, by_level(flux_weight), forcing_weight, tracer, land_sea,
    ]
    outs = pl.pallas_call(
        functools.partial(send_kernel, peers, levels, width, borders),
        out_shape=[sds((width, slots), bf16)]
        + [sds((width, slots + 256), bf16)] * len(borders)
        + [sds((width, 4 * OX), bf16)] * 2
        + [
            sds((2, width, columns), bf16), sds((width, OCELLS), f32), sds((2, OCELLS), i32),
            sds((1, OCELLS), f32), sds((3, slots), i32), sds((1, slots), f32),
            sds((size, blocks * vars_ + PAD, 128), f32),
        ],
        in_specs=[hbm] * 11,
        out_specs=[vmem] * (10 + len(borders)),
        scratch_shapes=[pltpu.SMEM(small[0].shape, f32)]
        + [pltpu.VMEM(x.shape, x.dtype) for x in small[1:8]]
        + [pltpu.VMEM((levels, OY + PAD, OX), f32), pltpu.VMEM(land_sea.shape, i32)]
        + [
            pltpu.VMEM((width, forcing_weight.shape[1]), f32),
            pltpu.SemaphoreType.DMA((len(small),)), pltpu.SemaphoreType.DMA((4,)),
        ],
        compiler_params=params,
        name="send",
    )(*[pltpu.with_memory_space_constraint(x, pltpu.HBM) for x in small + [state]])
    packed, sides = outs[0], outs[1 : 1 + len(borders)]
    even_t, odd_t, forcing_cols, t0, omap, oarea, smap, sarea, state = outs[1 + len(borders) :]
    got = []
    for mask in range(1, peers):
        buffer = sides[borders.index(mask)] if mask in borders else packed
        got.append(xor_swap(buffer, mask))

    first = [(i, i ^ 1) for i in range(tiles)]
    second = [(i, (i + 1) % tiles if i & 1 else (i - 1) % tiles) for i in range(tiles)]
    even_t, odd_t = swap(even_t, "atm", first), swap(odd_t, "atm", second)

    local = pl.pallas_call(
        functools.partial(local_kernel, width),
        out_shape=sds((width, OCELLS), f32),
        in_specs=[vmem] * 3, out_specs=vmem, compiler_params=params, name="local",
    )(forcing_cols, omap, oarea)

    slab = 24 * OX
    slabs = pl.pallas_call(
        functools.partial(slab_kernel, levels),
        out_shape=[sds((width, slab), f32), sds((8, slab), f32), sds((8, slab), f32)],
        in_specs=[vmem] * 3, out_specs=[vmem] * 3, compiler_params=params, name="slab",
    )(t0, even_t, odd_t)

    base, back_map = pl.pallas_call(
        functools.partial(state_kernel, levels),
        out_shape=[sds((vars_, size, columns), f32), sds((2 * vars_ * room, width), bf16)],
        in_specs=[vmem] * 4, out_specs=[vmem] * 2,
        scratch_shapes=[
            pltpu.VMEM((width, surface_map.shape[1]), f32),
            pltpu.VMEM((vars_, 2 * room, size), bf16),
        ],
        compiler_params=params, name="state",
    )(inverse, by_level(surface_weight), surface_map, state)

    send_rows = 5 * OX
    f_all, fs, ts, cmap, even, odd, edge = pl.pallas_call(
        functools.partial(receive_kernel, peers, levels, width, borders),
        out_shape=[
            sds((width, OCELLS), f32), sds((width, STRIPS * OX), f32),
            sds((width, STRIPS * OX), f32), sds((2, slots), i32),
            sds((width, send_rows), bf16), sds((width, send_rows), bf16),
            sds((width, 8 * OX), f32),
        ],
        in_specs=[anywhere] * 2 + [vmem] * (3 + peers), out_specs=[vmem] * 7,
        compiler_params=params, name="receive",
    )(slabs[2], back_map, packed, smap, local, t0, *got)
    even, odd = swap(even, "atm", first), swap(odd, "atm", second)

    dif = diffusivity.reshape(1, levels)
    scratch = lambda *shapes: [pltpu.VMEM(shape, f32) for shape in shapes]
    inner = pl.pallas_call(
        functools.partial(inner_kernel, levels, width),
        out_shape=sds((width, OCELLS), f32),
        in_specs=[vmem] * 5, out_specs=vmem,
        scratch_shapes=scratch(
            (width, STRIPS * OX), (8, OCELLS), (8, OCELLS), (8, STRIPS * OX), (8, STRIPS * OX),
            (width, OX),
        ),
        compiler_params=params, name="inner",
    )(f_all, fs, t0, ts, dif)
    t4, back = pl.pallas_call(
        functools.partial(outer_kernel, levels, width),
        out_shape=[sds((width, OCELLS), f32), sds((width, slots), bf16)],
        in_specs=[vmem] * 11, out_specs=[vmem] * 2,
        scratch_shapes=scratch(
            (width, slab), (width, 12 * OX), (8, 6 * OX), (8, 6 * OX), (width, OX),
        ),
        compiler_params=params, name="outer",
    )(f_all, t0, edge, inner, even, odd, *slabs, dif, cmap)

    returned = [xor_swap(back, mask) for mask in range(1, peers)]
    sums, tracer_out = pl.pallas_call(
        functools.partial(sum_kernel, levels, width),
        out_shape=[sds((width, columns), f32), pltpu.HBM(tracer.shape, f32)],
        in_specs=[vmem] * 3, out_specs=[vmem, hbm],
        scratch_shapes=[pltpu.VMEM((levels, OY + PAD, OX), f32), pltpu.SemaphoreType.DMA],
        compiler_params=params, name="sum",
    )(t4, omap, oarea)

    final_state = pl.pallas_call(
        functools.partial(final_kernel, peers, width),
        out_shape=pltpu.HBM((size, blocks * vars_, 128), f32),
        in_specs=[vmem] * (4 + peers), out_specs=hbm,
        scratch_shapes=[
            pltpu.VMEM((size, blocks * vars_ + PAD, 128), f32), pltpu.VMEM((width, columns), f32),
            pltpu.SemaphoreType.DMA((4,)),
        ],
        compiler_params=params, name="final",
    )(smap, sarea, sums, back_map, base, *returned)
    final_state = final_state.reshape(size, blocks, vars_, 128).transpose(2, 0, 1, 3)
    final_state = final_state.reshape(vars_, size, columns)
    return (final_state, tracer_out)


def solution(mesh):
    in_specs = (
        P(None, None, ("member", "atm", "ocn")),
        P("atm", None, None, None),
        P(),
        P(),
        P(),
        P(("atm", "ocn")),
        P(("atm", "ocn"), None),
        P(("atm", "ocn")),
        P(("atm", "ocn")),
        P(None, "atm", ("member", "ocn")),
        P("atm", "ocn"),
        P(),
        P(),
        P(),
    )
    out_specs = (P(None, None, ("member", "atm", "ocn")), P(None, "atm", ("member", "ocn")))
    return jax.shard_map(
        on_device, mesh=mesh, in_specs=in_specs, out_specs=out_specs, check_vma=False
    )
```

```python
import functools
import jax
import jax.numpy as jnp
from jax import lax
from jax.experimental import pallas as pl
from jax.experimental.pallas import tpu as pltpu
from jax.sharding import PartitionSpec as P

OSTEPS = 4
PAD = 8
NVAR = 4
OY = 32
OX = 128
OCELLS = OY * OX
STRIPS = 8
f32 = jnp.float32
bf16 = jnp.bfloat16
i32 = jnp.int32


def nn(a, b):
    return jnp.dot(a, b, preferred_element_type=f32)


def nt(a, b):
    return lax.dot_general(a, b, (((1,), (1,)), ((), ())), preferred_element_type=f32)


def split(x):
    high = x.astype(bf16)
    return high, (x - high.astype(f32)).astype(bf16)


def three(dot, a, b):
    ah, al = split(a)
    bh, bl = split(b)
    return dot(ah, bh) + dot(ah, bl) + dot(al, bh)


def doubled(x):
    return jnp.concatenate(list(split(x)), axis=0)


def wide(left, right, dot=nn):
    count = left.shape[0] // 2
    high, low = split(right)
    both = dot(left, high)
    return both[:count] + both[count:] + dot(left[:count], low)


def column_block(ref, var, first, blocks):
    size, rows, lanes = ref.shape
    lines = ref.reshape(size * rows, lanes)
    step = NVAR
    return jnp.concatenate(
        [lines[pl.ds((first + i) * step + var, size, stride=rows), :] for i in range(blocks)],
        axis=1,
    )


def iota(shape, dim):
    return lax.broadcasted_iota(i32, shape, dim)


def flat(x):
    return jnp.concatenate([x[i : i + 1, :] for i in range(x.shape[0])], axis=1)


def onehot(row, size):
    return jnp.where(iota((size, row.shape[1]), 0) == row, 1.0, 0.0).astype(bf16)


def place(high, low, payloads, rows):
    lines = iota((rows, high.shape[1]), 0) == high
    left = jnp.concatenate([jnp.where(lines, p, 0.0) for p in payloads], axis=0).astype(bf16)
    out = nt(left, onehot(low, 128))
    return [out[i * rows : (i + 1) * rows] for i in range(len(payloads))]


def stacked(x):
    return jnp.concatenate([x[:, h : h + 256] for h in range(0, x.shape[1], 256)], axis=0)


def two_terms(ref):
    return jnp.concatenate([stacked(ref[0]), stacked(ref[1])], axis=1)


def gather(source, low, high, width, chunk=512):
    count = source.shape[0] // width
    outs = []
    for start in range(0, low.shape[1], chunk):
        stop = min(start + chunk, low.shape[1])
        hot = onehot(low[:, start:stop], 256)
        if source.shape[1] == 512:
            hot = jnp.concatenate([hot, hot], axis=0)
        part = nn(source, hot)
        hc = high[:, start:stop]
        total = jnp.where(hc == 0, part[:width], 0.0)
        for h in range(1, count):
            total = jnp.where(hc == h, part[h * width : (h + 1) * width], total)
        outs.append(total)
    return outs[0] if len(outs) == 1 else jnp.concatenate(outs, axis=1)


def spread(value, low, high, count):
    parts = [jnp.where(high == h, value, 0.0) for h in range(count)]
    return nt(jnp.concatenate(parts, axis=0).astype(bf16), onehot(low, 256))


def pick(level_rows, lane_rows, base):
    index = iota(level_rows.shape, 0)
    for i, row in enumerate(lane_rows):
        level_rows = jnp.where(index == base + i, row, level_rows)
    return level_rows


def roll(x, shift):
    shift = shift % 128
    return x if shift == 0 else pltpu.roll(x, shift, 1)


def row_of(x, y):
    return x[:, y * OX : (y + 1) * OX]


def border_block(x, lane):
    blocks = []
    for i in range(2):
        block = jnp.zeros((x.shape[0], OX), f32)
        for b in range(4):
            for j in range(4):
                first = b * 32 + j * 8
                moved = roll(row_of(x, b * 8 + i * 4 + j), first + 4)
                block = jnp.where((lane >= first) & (lane < first + 8), moved, block)
        blocks.append(block)
    return jnp.concatenate(blocks, axis=1)


def strips(x, halo, lane):
    outs = []
    for j in range(STRIPS):
        side = roll(row_of(halo, j // 4), 8 - (j % 4) * 8)
        for b in range(4):
            line = row_of(x, b * 8 + j)
            first = b * 32
            side = jnp.where((lane >= first) & (lane < first + 8), roll(line, first + 8), side)
            side = jnp.where(
                (lane >= first + 16) & (lane < first + 24), roll(line, first + 16), side
            )
        outs.append(side)
    return outs


def send_kernel(
    peers, levels, width, borders,
    *refs,
):
    sources, rest = refs[:11], refs[11:]
    packed_ref, rest = rest[0], rest[1:]
    side_refs, rest = rest[: len(borders)], rest[len(borders) :]
    (even_ref, odd_ref), rest = rest[:2], rest[2:]
    forcing_ref, t_ref, omap_ref, oarea_ref, smap_ref, sarea_ref, state_ref = rest[:7]
    staged, fw_pad, sems, state_sems = rest[7:17], rest[17], rest[18], rest[19]
    (area_ref, col_ref, dest_ref, cell_ref, class_ref, inv_ref, flux_ref, fw_ref, tracer_ref,
     land_ref) = staged
    loads = [
        pltpu.make_async_copy(a, b.at[:, pl.ds(0, OY), :] if b is tracer_ref else b, sems.at[i])
        for i, (a, b) in enumerate(zip(sources[:10], staged))
    ]
    for load in loads:
        load.start()
    state_hbm = sources[10]
    parts = state_sems.shape[0]
    part_rows = state_hbm.shape[1] // parts
    state_loads = []
    for i in range(parts):
        at = pl.ds(i * part_rows, part_rows)
        state_loads.append(
            pltpu.make_async_copy(
                state_hbm.at[:, at, :], state_ref.at[:, at, :], state_sems.at[i]
            )
        )
        state_loads[i].start()
    for load in loads[:5]:
        load.wait()
    me = lax.axis_index("ocn")
    slots = packed_ref.shape[1]
    slot_rows = slots // 128
    slot_pad = -(-slot_rows // 8) * 8
    lines = col_ref.shape[0]
    lane = iota((1, 128), 1)

    offset = (dest_ref[...] - me) & (peers - 1)
    cells = cell_ref[...]
    classes = class_ref[...]
    cols = col_ref[...]
    area = jnp.zeros(cols.shape, f32)
    for i in range(area_ref.shape[0]):
        area = jnp.where(classes == i, area_ref[i], area)

    hits = [jnp.where(offset == k, 1.0, 0.0) for k in range(1, peers)]
    hot = jnp.concatenate(hits, axis=0)
    upper = jnp.where(iota((128, 128), 0) <= iota((128, 128), 1), 1.0, 0.0).astype(bf16)
    running = nn(hot.astype(bf16), upper)
    count = running.shape[0]
    totals = jnp.broadcast_to(running[:, 127:128], running.shape).astype(bf16)
    below = jnp.where(iota((count, count), 1) < iota((count, count), 0), 1.0, 0.0).astype(bf16)
    before = nn(below, totals)
    place_of = running + before - 1.0
    slot = jnp.full(cols.shape, -1.0, f32)
    for k in range(1, peers):
        at = (k - 1) * lines
        slot = jnp.where(offset == k, place_of[at : at + lines], slot)
    slot = slot.astype(i32)
    position = iota((slot_pad, 128), 0) * 128 + iota((slot_pad, 128), 1)
    segment = jnp.full((slot_pad, 128), 1, i32)
    for k in range(2, peers):
        at = (k - 1) * lines
        start = before[at : at + 1, :].astype(i32)
        segment = segment + jnp.where(position >= start, 1, 0)

    a1 = area.astype(bf16).astype(f32)
    a2 = (area - a1).astype(bf16).astype(f32)
    a3 = area - a1 - a2
    slot_f, cell_f = flat(slot), flat(cells)
    col_f = flat(cols)
    areas = [flat(a1), flat(a2), flat(a3)]
    col_low = (col_f & 255).astype(f32)
    col_high = lax.shift_right_arithmetic(col_f, 8).astype(f32)
    cell_low = cell_f & 127
    cell_high = lax.shift_right_arithmetic(cell_f, 7)
    got = place(
        lax.shift_right_arithmetic(slot_f, 7), slot_f & 127,
        [col_low, col_high] + areas + [cell_high.astype(f32), cell_low.astype(f32)], slot_pad,
    )
    keep = [flat(g[:slot_rows]) for g in got]
    s_low, s_high = keep[0].astype(i32), keep[1].astype(i32)
    s_area = keep[2] + keep[3] + keep[4]
    smap_ref[0:1, :] = s_low
    smap_ref[1:2, :] = s_high
    smap_ref[2:3, :] = flat(segment[:slot_rows])
    sarea_ref[...] = s_area

    local_high = jnp.where(flat(offset) == 0, cell_high, -1)
    own = place(local_high, cell_low, [col_low, col_high + 1.0] + areas, OY)
    o_low, o_high = own[0].astype(i32), own[1].astype(i32) - 1
    o_area = own[2] + own[3] + own[4]
    omap_ref[0:1, :] = flat(o_low)
    omap_ref[1:2, :] = flat(o_high)
    oarea_ref[...] = flat(o_area)

    blank = jnp.zeros((2, 128), f32)
    edge = []
    for m in (own[0], own[1], o_area):
        block = blank
        for b in range(4):
            part = m[b * 8 : (b + 1) * 8]
            for j in range(4):
                first = b * 32 + j * 8
                moved = roll(part, first + 4)
                pair = jnp.concatenate([moved[j : j + 1], moved[4 + j : 5 + j]], axis=0)
                block = jnp.where((lane >= first) & (lane < first + 8), pair, block)
        edge.append(flat(block))

    for load in loads[5:]:
        load.wait()
    fw_pad[...] = jnp.zeros_like(fw_pad)
    fw_pad[0:levels, :] = fw_ref[...]
    fw = fw_pad[...]
    size = inv_ref.shape[0]
    flux = flux_ref[...].reshape(size * NVAR, flux_ref.shape[2])
    mixed = wide(doubled(fw), flux, nt)
    which = iota((1, size * NVAR), 1) & (NVAR - 1)
    masked = jnp.concatenate([jnp.where(which == v, mixed, 0.0) for v in range(NVAR)], axis=0)
    drawn = wide(doubled(masked), inv_ref[...].reshape(size * NVAR, size))
    pulled = [doubled(drawn[v * width : (v + 1) * width]) for v in range(NVAR)]

    tracer_lines = tracer_ref.reshape(levels * (OY + PAD), OX)
    for y in range(OY):
        at = pl.ds(y * OX, OX)
        t_ref[0:levels, at] = tracer_lines[pl.ds(y, levels, stride=OY + PAD), :]
        t_ref[levels : levels + 1, at] = land_ref[y : y + 1, :].astype(f32)
        t_ref[levels + 1 : width, at] = jnp.zeros((width - levels - 1, OX), f32)

    is_even = (lax.axis_index("atm") & 1) == 0
    top, bottom = t_ref[:, 0 : 4 * OX], t_ref[:, 28 * OX : 32 * OX]
    even_ref[...] = jnp.where(is_even, bottom, top).astype(bf16)
    odd_ref[...] = jnp.where(is_even, top, bottom).astype(bf16)

    for i in range(parts):
        state_loads[i].wait()
        for c in range(i * part_rows // NVAR, (i + 1) * part_rows // NVAR, 2):
            total = None
            for v in range(NVAR):
                term = wide(pulled[v], column_block(state_ref, v, c, 2))
                total = term if total is None else total + term
            at = slice(c * 128, (c + 2) * 128)
            forcing_ref[0, :, at], forcing_ref[1, :, at] = split(total)
    source = two_terms(forcing_ref)

    rows = gather(source, s_low, s_high, width) * s_area
    rows = pick(rows, keep[5:7], levels + 1).astype(bf16)
    packed_ref[...] = rows
    f_edge = gather(source, edge[0].astype(i32), edge[1].astype(i32) - 1, width) * edge[2]
    t_edge = border_block(t_ref[...], lane)
    lead = (lane & 7) < 4
    to_right, to_left = [], []
    for i in range(2):
        fe, te = row_of(f_edge, i), row_of(t_edge, i)
        to_right.append(jnp.where(lead, fe, roll(te, 4)))
        to_left.append(jnp.where(lead, roll(fe, -4), te))
    to_right = jnp.concatenate(to_right, axis=1)
    to_left = jnp.concatenate(to_left, axis=1)
    for mask, ref in zip(borders, side_refs):
        ref[:, 0:slots] = rows
        ref[:, slots : slots + 256] = jnp.where((me ^ mask) == me + 1, to_right, to_left).astype(
            bf16
        )


def local_kernel(width, forcing_ref, omap_ref, oarea_ref, out_ref):
    source = two_terms(forcing_ref)
    out_ref[...] = gather(source, omap_ref[0:1, :], omap_ref[1:2, :], width) * oarea_ref[...]


def receive_kernel(
    peers, levels, width, borders, early0, early1, packed_ref, smap_ref, local_ref, t_ref, *rest
):
    got = rest[: peers - 1]
    f_ref, fs_ref, ts_ref, cmap_ref, even_ref, odd_ref, edge_ref = rest[peers - 1 :]
    me = lax.axis_index("ocn")
    slots = packed_ref.shape[1]
    lane = iota((1, 128), 1)
    segment = smap_ref[2:3, :]
    chunks = slots // 256

    def meant_for(tile):
        total = jnp.zeros((width, slots), f32)
        for mask in range(peers):
            ref = packed_ref if mask == 0 else got[mask - 1]
            step = (tile - (me ^ mask)) & (peers - 1)
            total = jnp.where(segment == step, ref[:, 0:slots].astype(f32), total)
        high = total[levels + 1 : levels + 2, :].astype(i32)
        low = total[levels + 2 : levels + 3, :].astype(i32)
        return stacked(total.astype(bf16)), high, low

    index = iota((1, slots), 1)
    payload = [(index & 255).astype(f32), (lax.shift_right_arithmetic(index, 8) + 1).astype(f32)]

    source, high, low = meant_for(me)
    cell = high * 128 + low
    cmap_ref[0:1, :] = cell & 255
    cmap_ref[1:2, :] = lax.shift_right_arithmetic(cell, 8)
    where_low, where_high = place(high, low, payload, OY)
    f_ref[...] = local_ref[...] + gather(
        source, flat(where_low).astype(i32), flat(where_high).astype(i32) - 1, width
    )

    halo_f = None
    for step in (-1, 1):
        source, high, low = meant_for(me + step)
        at = low - 120 if step < 0 else low
        inside = (low >= 124) if step < 0 else (low < 4)
        block = lax.shift_right_arithmetic(high & 7, 2)
        spot = lax.shift_right_arithmetic(high, 3) * 32 + (high & 3) * 8 + at
        where_low, where_high = place(jnp.where(inside, block, -1), spot, payload, 8)
        part = gather(
            source, flat(where_low[:2]).astype(i32), flat(where_high[:2]).astype(i32) - 1, width
        )
        halo_f = part if halo_f is None else halo_f + part

    def side_from(tile):
        block = jnp.zeros((width, 256), f32)
        for mask in borders:
            block = jnp.where(
                (me ^ mask) == tile, got[mask - 1][:, slots : slots + 256].astype(f32), block
            )
        return block

    from_left, from_right = side_from(me - 1), side_from(me + 1)
    lead = (lane & 7) < 4
    side_f, side_t = [], []
    for i in range(2):
        fl, fr = row_of(from_left, i), row_of(from_right, i)
        side_f.append(jnp.where(lead, fr, roll(fl, 4)) + row_of(halo_f, i))
        side_t.append(jnp.where(lead, roll(fr, -4), fl))
    f_strips = strips(f_ref[...], jnp.concatenate(side_f, axis=1), lane)
    t_strips = strips(t_ref[...], jnp.concatenate(side_t, axis=1), lane)
    for j in range(STRIPS):
        fs_ref[:, j * OX : (j + 1) * OX] = f_strips[j]
        ts_ref[:, j * OX : (j + 1) * OX] = t_strips[j]

    def four(parts, first, source):
        block = jnp.zeros((width, OX), f32)
        for m in range(4):
            inside = (lane >= m * 32) & (lane < m * 32 + 32)
            block = jnp.where(inside, roll(parts[first + m], 32 * (m - source)), block)
        return block

    edges = [four(p, first, source) for p in (f_strips, t_strips)
             for first, source in ((0, 0), (4, 0), (0, 3), (4, 3))]
    edge_ref[...] = jnp.concatenate(edges, axis=1)
    top = jnp.concatenate([f_ref[:, 0 : 3 * OX], edges[0], edges[4]], axis=1)
    bottom = jnp.concatenate([f_ref[:, 29 * OX : 32 * OX], edges[3], edges[7]], axis=1)
    is_even = (lax.axis_index("atm") & 1) == 0
    even_ref[...] = jnp.where(is_even, bottom, top).astype(bf16)
    odd_ref[...] = jnp.where(is_even, top, bottom).astype(bf16)


def tile_row(ref, y):
    return ref[:, y * OX : (y + 1) * OX]


def not_there(lane):
    me, peers = lax.axis_index("ocn"), lax.axis_size("ocn")
    spot = lane & 31
    return ((me == 0) & (spot >= 12) & (spot < 16)) | (
        (me == peers - 1) & (spot >= 8) & (spot < 12)
    )


def fill_diffusivity(ref, dif_ref):
    width, levels = ref.shape[0], dif_ref.shape[1]
    diag = iota((width, levels), 0) == iota((width, levels), 1)
    column = jnp.sum(jnp.where(diag, dif_ref[...], 0.0), axis=1, keepdims=True)
    ref[...] = jnp.broadcast_to(column, ref.shape)


def count_rows(w8, n8, rows):
    for y in rows:
        here = tile_row(w8, y)
        n8[:, y * OX : (y + 1) * OX] = (
            tile_row(w8, y - 1) + tile_row(w8, y + 1) + roll(here, 1) + roll(here, -1)
        )


def substep_rows(rows, forcing, wet, counts, dif):
    for step in range(OSTEPS):
        new = list(rows)
        for y in range(step + 1, len(rows) - 1 - step):
            here = rows[y]
            lap = (rows[y - 1] + rows[y + 1] - counts(y) * here) + (roll(here, 1) + roll(here, -1))
            new[y] = here + wet(y) * (dif * lap + forcing(y))
        rows = new
    return rows


def substep_strips(now, forcing, wet, counts, dif, ends):
    for step in range(OSTEPS):
        new = []
        for j, here in enumerate(now):
            up, down = ends(now, j)
            lap = (roll(here, 1) + roll(here, -1) - counts[j] * here) + (up + down)
            new.append(here + wet[j] * (dif * lap + forcing[j]))
        now = new
    return now


def tall(ref, j, count):
    return jnp.concatenate([tile_row(ref, j)] * (count // 8), axis=0)


def merged(line, value, lane, b):
    value = jnp.where(lane < 4, roll(line, -(b * 32 + 16)), value)
    return jnp.where(lane >= 124, roll(line, 120 - b * 32), value)


def inner_kernel(
    levels, width, f_ref, fs_ref, t_ref, ts_ref, dif_ref, tt_ref, strip, w8, n8, ws8, ns8, d8
):
    lane = iota((1, 128), 1)
    w8[...] = jnp.broadcast_to(t_ref[levels : levels + 1, :], w8.shape)
    count_rows(w8, n8, range(1, OY - 1))
    outside = not_there(lane)
    for j in range(STRIPS):
        line = tile_row(ts_ref, j)[levels : levels + 1, :]
        ws8[:, j * OX : (j + 1) * OX] = jnp.broadcast_to(jnp.where(outside, 0.0, line), (8, OX))

    def ends(parts, j):
        up = roll(parts[STRIPS - 1], 32) if j == 0 else parts[j - 1]
        down = roll(parts[0], 96) if j == STRIPS - 1 else parts[j + 1]
        return up, down

    parts = [tile_row(ws8, j) for j in range(STRIPS)]
    for j in range(STRIPS):
        up, down = ends(parts, j)
        ns8[:, j * OX : (j + 1) * OX] = up + down + roll(parts[j], 1) + roll(parts[j], -1)
    fill_diffusivity(d8, dif_ref)

    lev = slice(0, width)

    def strip_group():

        def load(ref, j):
            return ref[lev, j * OX : (j + 1) * OX]

        wet = [tall(ws8, j, width) for j in range(STRIPS)]
        now = substep_strips(
            [load(ts_ref, j) * wet[j] for j in range(STRIPS)],
            [load(fs_ref, j) for j in range(STRIPS)], wet,
            [tall(ns8, j, width) for j in range(STRIPS)], d8[lev, :], ends,
        )
        for j in range(STRIPS):
            strip[lev, j * OX : (j + 1) * OX] = now[j]

    strip_group()

    def main():
        dif = d8[lev, :]

        def load(ref, j):
            return ref[lev, j * OX : (j + 1) * OX]

        rows = substep_rows(
            [load(t_ref, y) * tall(w8, y, width) for y in range(OY)], lambda y: load(f_ref, y),
            lambda y: tall(w8, y, width), lambda y: tall(n8, y, width), dif,
        )
        now = [load(strip, j) for j in range(STRIPS)]
        for y in range(4, OY - 4):
            value = merged(now[y % 8], rows[y], lane, y // 8)
            tt_ref[lev, y * OX : (y + 1) * OX] = jnp.where(
                tall(w8, y, width) > 0.0, value, load(t_ref, y)
            )

    main()


def slab_kernel(levels, t_ref, even_ref, odd_ref, s, w8, n8):
    row, rows_atm = lax.axis_index("atm"), lax.axis_size("atm")
    is_even = (row & 1) == 0
    even, odd = even_ref[...].astype(f32), odd_ref[...].astype(f32)
    top, bottom = jnp.where(is_even, odd, even), jnp.where(is_even, even, odd)
    tops = jnp.where(row > 0, 1.0, 0.0)
    bottoms = jnp.where(row < rows_atm - 1, 1.0, 0.0)

    def wide_wet(x):
        return jnp.broadcast_to(x[levels : levels + 1, :], (8, x.shape[1]))

    w8[:, 0 : 4 * OX] = wide_wet(top) * tops
    w8[:, 4 * OX : 12 * OX] = wide_wet(t_ref[:, 0 : 8 * OX])
    w8[:, 12 * OX : 20 * OX] = wide_wet(t_ref[:, 24 * OX : 32 * OX])
    w8[:, 20 * OX : 24 * OX] = wide_wet(bottom) * bottoms
    for y in (0, 11, 12, 23):
        n8[:, y * OX : (y + 1) * OX] = jnp.zeros((8, OX), f32)
    count_rows(w8, n8, list(range(1, 11)) + list(range(13, 23)))
    s[:, 0 : 4 * OX] = top * w8[0:1, 0 : 4 * OX]
    s[:, 4 * OX : 12 * OX] = t_ref[:, 0 : 8 * OX] * w8[0:1, 4 * OX : 12 * OX]
    s[:, 12 * OX : 20 * OX] = t_ref[:, 24 * OX : 32 * OX] * w8[0:1, 12 * OX : 20 * OX]
    s[:, 20 * OX : 24 * OX] = bottom * w8[0:1, 20 * OX : 24 * OX]


def outer_kernel(
    levels, width,
    f_ref, t_ref, edge_ref, inner_ref, even_ref, odd_ref, s, w8, n8, dif_ref, cmap_ref,
    tt_ref, back_ref,
    fx, se, we8, ne8, d8,
):
    row, rows_atm = lax.axis_index("atm"), lax.axis_size("atm")
    is_even = (row & 1) == 0
    lane = iota((1, 128), 1)
    block = lax.shift_right_arithmetic(lane, 5)
    even, odd = even_ref[...].astype(f32), odd_ref[...].astype(f32)
    top, bottom = jnp.where(is_even, odd, even), jnp.where(is_even, even, odd)
    tops = jnp.where(row > 0, 1.0, 0.0)
    bottoms = jnp.where(row < rows_atm - 1, 1.0, 0.0)

    def wide_wet(x):
        return jnp.broadcast_to(x[levels : levels + 1, :], (8, x.shape[1]))

    fx[:, OX : 4 * OX] = top[:, 0 : 3 * OX]
    fx[:, 4 * OX : 12 * OX] = f_ref[:, 0 : 8 * OX]
    fx[:, 12 * OX : 20 * OX] = f_ref[:, 24 * OX : 32 * OX]
    fx[:, 20 * OX : 23 * OX] = bottom[:, 0 : 3 * OX]
    outside = not_there(lane)
    for at, f_part, t_part, there in (
        (0, top[:, 384:512], top[:, 512:640], tops),
        (1, edge_ref[:, 0:128], edge_ref[:, 512:640], None),
        (2, edge_ref[:, 128:256], edge_ref[:, 640:768], None),
        (3, edge_ref[:, 256:384], edge_ref[:, 768:896], None),
        (4, edge_ref[:, 384:512], edge_ref[:, 896:1024], None),
        (5, bottom[:, 384:512], bottom[:, 512:640], bottoms),
    ):
        wet = jnp.where(outside, 0.0, wide_wet(t_part))
        wet = wet if there is None else wet * there
        we8[:, at * OX : (at + 1) * OX] = wet
        se[:, at * OX : (at + 1) * OX] = t_part * wet[0:1, :]
        se[:, (6 + at) * OX : (7 + at) * OX] = f_part

    def ends(parts, j):
        before = parts[j] if j % 3 == 0 else jnp.where(block == 3, parts[j - 1], parts[j])
        after = parts[j] if j % 3 == 2 else jnp.where(block == 0, parts[j + 1], parts[j])
        return roll(before, 32), roll(after, 96)

    parts = [tile_row(we8, j) for j in range(6)]
    for j in range(6):
        up, down = ends(parts, j)
        ne8[:, j * OX : (j + 1) * OX] = up + down + roll(parts[j], 1) + roll(parts[j], -1)
    fill_diffusivity(d8, dif_ref)
    tt_ref[:, 4 * OX : 28 * OX] = inner_ref[:, 4 * OX : 28 * OX]

    lev = slice(0, width)

    def strip_group():

        def load(ref, j):
            return ref[lev, j * OX : (j + 1) * OX]

        now = substep_strips(
            [load(se, j) for j in range(6)], [load(se, 6 + j) for j in range(6)],
            [tall(we8, j, width) for j in range(6)], [tall(ne8, j, width) for j in range(6)],
            d8[lev, :], ends,
        )
        se[lev, 0:OX], se[lev, OX : 2 * OX] = now[1], now[4]

    strip_group()

    def main():
        dif = d8[lev, :]

        def load(ref, j):
            return ref[lev, j * OX : (j + 1) * OX]

        slabs = []
        for base in (0, 12):
            slabs += substep_rows(
                [load(s, base + y) for y in range(12)], lambda y: load(fx, base + y),
                lambda y: tall(w8, base + y, width), lambda y: tall(n8, base + y, width), dif,
            )
        for m in range(4):
            for y, slab, line in ((m, 4 + m, load(se, 0)), (28 + m, 16 + m, load(se, 1))):
                value = merged(line, slabs[slab], lane, m)
                tt_ref[lev, y * OX : (y + 1) * OX] = jnp.where(
                    tall(w8, slab, width) > 0.0, value, load(t_ref, y)
                )

    main()
    source = stacked(tt_ref[...].astype(bf16))
    back_ref[...] = gather(source, cmap_ref[0:1, :], cmap_ref[1:2, :], width).astype(bf16)


def state_kernel(levels, inv_ref, sw_ref, sm_ref, state_ref, out_ref, h_ref, sm_pad, square):
    sm_pad[...] = jnp.zeros_like(sm_pad)
    sm_pad[0:levels, :] = sm_ref[...]
    h_ref[...] = jnp.zeros_like(h_ref)
    square[...] = jnp.zeros_like(square)
    blocks = (state_ref.shape[1] - PAD) // NVAR
    size = inv_ref.shape[0]
    room = h_ref.shape[0] // (2 * NVAR)
    for v in range(NVAR):
        inv = inv_ref[:, v, :]
        high, low = split(three(nn, inv, three(nt, sw_ref[:, v, :], sm_pad[...])))
        h_ref[v * room : v * room + size, :] = high
        h_ref[(NVAR + v) * room : (NVAR + v) * room + size, :] = low
        if v < NVAR - 1:
            square[v, 0:size, :], square[v, room : room + size, :] = split(three(nn, inv, inv))
    for v in range(NVAR - 1):
        for c in range(0, blocks, 2):
            value = wide(square[v], column_block(state_ref, v, c, 2))
            out_ref[v, :, c * 128 : (c + 2) * 128] = value[:size]


def late_state_kernel(after, inv_ref, state_ref, out_ref, square):
    square[...] = jnp.zeros_like(square)
    blocks = (state_ref.shape[1] - PAD) // NVAR
    size = inv_ref.shape[0]
    room = square.shape[0] // 2
    last = NVAR - 1
    inv = inv_ref[:, last, :]
    square[0:size, :], square[room : room + size, :] = split(three(nn, inv, inv))
    for c in range(0, blocks, 2):
        value = wide(square[...], column_block(state_ref, last, c, 2))
        out_ref[:, c * 128 : (c + 2) * 128] = value[:size]


def sum_kernel(levels, width, tt_ref, omap_ref, oarea_ref, out_ref, tracer_hbm, rows, sem):
    lines = rows.reshape(levels * (OY + PAD), OX)
    for y in range(OY):
        lines[pl.ds(y, levels, stride=OY + PAD), :] = tt_ref[0:levels, y * OX : (y + 1) * OX]
    store = pltpu.make_async_copy(rows.at[:, pl.ds(0, OY), :], tracer_hbm, sem)
    store.start()
    count = out_ref.shape[1] // 256
    chunk = 1024
    total = None
    for start in range(0, OCELLS, chunk):
        at = slice(start, start + chunk)
        value = tt_ref[:, at] * oarea_ref[:, at]
        value, rest = (term.astype(f32) for term in split(value))
        part = spread(value, omap_ref[0:1, at], omap_ref[1:2, at], count)
        part = part + spread(rest, omap_ref[0:1, at], omap_ref[1:2, at], count)
        total = part if total is None else total + part
    for h in range(count):
        out_ref[:, h * 256 : (h + 1) * 256] = total[h * width : (h + 1) * width]
    store.wait()


def final_kernel(
    peers, width, smap_ref, sarea_ref, sum_ref, h_ref, base_ref, last_ref, *rest
):
    got = rest[: peers - 1]
    out_hbm, rows, sums, sems = rest[peers - 1 :]
    columns = sum_ref.shape[1]
    count = columns // 256
    me = lax.axis_index("ocn")
    segment = smap_ref[2:3, :]
    total = jnp.zeros((width, segment.shape[1]), f32)
    for mask in range(1, peers):
        offset = ((me ^ mask) - me) & (peers - 1)
        total = jnp.where(segment == offset, got[mask - 1][...].astype(f32), total)
    part = spread(total * sarea_ref[...], smap_ref[0:1, :], smap_ref[1:2, :], count)
    for h in range(count):
        at = slice(h * 256, (h + 1) * 256)
        sums[:, at] = part[h * width : (h + 1) * width] + sum_ref[:, at]

    size, stride, lanes = rows.shape
    lines = rows.reshape(size * stride, lanes)
    parts = sems.shape[0]
    room = h_ref.shape[0] // (2 * NVAR)
    stores = []
    for i in range(parts):
        share = columns // parts
        for c in range(i * share, (i + 1) * share, 256):
            every = wide(h_ref[...], sums[:, c : c + 256])
            for v in range(NVAR):
                at = slice(c, c + 256)
                base = base_ref[v, :, at] if v < NVAR - 1 else last_ref[:, at]
                value = base + every[v * room : v * room + size]
                for k in range(2):
                    first = (c // 128 + k) * NVAR + v
                    lines[pl.ds(first, size, stride=stride), :] = value[:, k * 128 : k * 128 + 128]
        at = pl.ds(i * (share // 128 * NVAR), share // 128 * NVAR)
        store = pltpu.make_async_copy(rows.at[:, at, :], out_hbm.at[:, at, :], sems.at[i])
        store.start()
        stores.append(store)
    for store in stores:
        store.wait()


def on_device(
    atmos_state, inverses, flux_weight, surface_weight, area_table, xc_column, xc_dest, xc_cell,
    xc_class, tracer, land_sea, forcing_weight, surface_map, diffusivity,
):
    peers, tiles = lax.axis_size("ocn"), lax.axis_size("atm")
    vars_, size, columns = atmos_state.shape
    cells = xc_column.shape[0]
    levels = tracer.shape[0]
    slots = cells - 3 * cells // peers
    width = -(-(levels + 3) // 16) * 16
    borders = sorted({i ^ (i + 1) for i in range(peers - 1)})
    sds = jax.ShapeDtypeStruct
    params = pltpu.CompilerParams(vmem_limit_bytes=30 * 1024 * 1024)
    vmem = pl.BlockSpec(memory_space=pltpu.VMEM)

    def swap(x, axis, pairs):
        return lax.ppermute(x, axis, pairs)

    def xor_swap(x, mask):
        return swap(x, "ocn", [(i, i ^ mask) for i in range(peers)])

    blocks = columns // 128
    room = -(-size // 16) * 16
    by_level = lambda x: x.transpose(1, 0, 2)
    state = atmos_state.reshape(vars_, size, blocks, 128).transpose(1, 2, 0, 3)
    state = state.reshape(size, blocks * vars_, 128)
    inverse = by_level(inverses[0])
    hbm = pl.BlockSpec(memory_space=pltpu.HBM)
    anywhere = pl.BlockSpec(memory_space=pl.ANY)
    grid_of = lambda x: x.reshape(cells // 128, 128)
    small = [
        area_table, grid_of(xc_column), grid_of(xc_dest), grid_of(xc_cell), grid_of(xc_class),
        inverse, by_level(flux_weight), forcing_weight, tracer, land_sea,
    ]
    outs = pl.pallas_call(
        functools.partial(send_kernel, peers, levels, width, borders),
        out_shape=[sds((width, slots), bf16)]
        + [sds((width, slots + 256), bf16)] * len(borders)
        + [sds((width, 4 * OX), bf16)] * 2
        + [
            sds((2, width, columns), bf16), sds((width, OCELLS), f32), sds((2, OCELLS), i32),
            sds((1, OCELLS), f32), sds((3, slots), i32), sds((1, slots), f32),
            sds((size, blocks * vars_ + PAD, 128), f32),
        ],
        in_specs=[hbm] * 11,
        out_specs=[vmem] * (10 + len(borders)),
        scratch_shapes=[pltpu.SMEM(small[0].shape, f32)]
        + [pltpu.VMEM(x.shape, x.dtype) for x in small[1:8]]
        + [pltpu.VMEM((levels, OY + PAD, OX), f32), pltpu.VMEM(land_sea.shape, i32)]
        + [
            pltpu.VMEM((width, forcing_weight.shape[1]), f32),
            pltpu.SemaphoreType.DMA((len(small),)), pltpu.SemaphoreType.DMA((4,)),
        ],
        compiler_params=params,
        name="send",
    )(*[pltpu.with_memory_space_constraint(x, pltpu.HBM) for x in small + [state]])
    packed, sides = outs[0], outs[1 : 1 + len(borders)]
    even_t, odd_t, forcing_cols, t0, omap, oarea, smap, sarea, state = outs[1 + len(borders) :]
    got = []
    for mask in range(1, peers):
        buffer = sides[borders.index(mask)] if mask in borders else packed
        got.append(xor_swap(buffer, mask))

    first = [(i, i ^ 1) for i in range(tiles)]
    second = [(i, (i + 1) % tiles if i & 1 else (i - 1) % tiles) for i in range(tiles)]
    even_t, odd_t = swap(even_t, "atm", first), swap(odd_t, "atm", second)

    local = pl.pallas_call(
        functools.partial(local_kernel, width),
        out_shape=sds((width, OCELLS), f32),
        in_specs=[vmem] * 3, out_specs=vmem, compiler_params=params, name="local",
    )(forcing_cols, omap, oarea)

    slab = 24 * OX
    slabs = pl.pallas_call(
        functools.partial(slab_kernel, levels),
        out_shape=[sds((width, slab), f32), sds((8, slab), f32), sds((8, slab), f32)],
        in_specs=[vmem] * 3, out_specs=[vmem] * 3, compiler_params=params, name="slab",
    )(t0, even_t, odd_t)

    base, back_map = pl.pallas_call(
        functools.partial(state_kernel, levels),
        out_shape=[sds((vars_ - 1, size, columns), f32), sds((2 * vars_ * room, width), bf16)],
        in_specs=[vmem] * 4, out_specs=[vmem] * 2,
        scratch_shapes=[
            pltpu.VMEM((width, surface_map.shape[1]), f32),
            pltpu.VMEM((vars_ - 1, 2 * room, size), bf16),
        ],
        compiler_params=params, name="state",
    )(inverse, by_level(surface_weight), surface_map, state)

    send_rows = 5 * OX
    f_all, fs, ts, cmap, even, odd, edge = pl.pallas_call(
        functools.partial(receive_kernel, peers, levels, width, borders),
        out_shape=[
            sds((width, OCELLS), f32), sds((width, STRIPS * OX), f32),
            sds((width, STRIPS * OX), f32), sds((2, slots), i32),
            sds((width, send_rows), bf16), sds((width, send_rows), bf16),
            sds((width, 8 * OX), f32),
        ],
        in_specs=[anywhere] * 2 + [vmem] * (3 + peers), out_specs=[vmem] * 7,
        compiler_params=params, name="receive",
    )(slabs[2], back_map, packed, smap, local, t0, *got)
    even, odd = swap(even, "atm", first), swap(odd, "atm", second)

    dif = diffusivity.reshape(1, levels)
    scratch = lambda *shapes: [pltpu.VMEM(shape, f32) for shape in shapes]
    inner = pl.pallas_call(
        functools.partial(inner_kernel, levels, width),
        out_shape=sds((width, OCELLS), f32),
        in_specs=[vmem] * 5, out_specs=vmem,
        scratch_shapes=scratch(
            (width, STRIPS * OX), (8, OCELLS), (8, OCELLS), (8, STRIPS * OX), (8, STRIPS * OX),
            (width, OX),
        ),
        compiler_params=params, name="inner",
    )(f_all, fs, t0, ts, dif)
    t4, back = pl.pallas_call(
        functools.partial(outer_kernel, levels, width),
        out_shape=[sds((width, OCELLS), f32), sds((width, slots), bf16)],
        in_specs=[vmem] * 11, out_specs=[vmem] * 2,
        scratch_shapes=scratch(
            (width, slab), (width, 12 * OX), (8, 6 * OX), (8, 6 * OX), (width, OX),
        ),
        compiler_params=params, name="outer",
    )(f_all, t0, edge, inner, even, odd, *slabs, dif, cmap)

    returned = [xor_swap(back, mask) for mask in range(1, peers)]
    sums, tracer_out = pl.pallas_call(
        functools.partial(sum_kernel, levels, width),
        out_shape=[sds((width, columns), f32), pltpu.HBM(tracer.shape, f32)],
        in_specs=[vmem] * 3, out_specs=[vmem, hbm],
        scratch_shapes=[pltpu.VMEM((levels, OY + PAD, OX), f32), pltpu.SemaphoreType.DMA],
        compiler_params=params, name="sum",
    )(t4, omap, oarea)

    last = pl.pallas_call(
        late_state_kernel,
        out_shape=sds((size, columns), f32),
        in_specs=[anywhere] + [vmem] * 2, out_specs=vmem,
        scratch_shapes=[pltpu.VMEM((2 * room, size), bf16)],
        compiler_params=params, name="late_state",
    )(back, inverse, state)

    final_state = pl.pallas_call(
        functools.partial(final_kernel, peers, width),
        out_shape=pltpu.HBM((size, blocks * vars_, 128), f32),
        in_specs=[vmem] * (5 + peers), out_specs=hbm,
        scratch_shapes=[
            pltpu.VMEM((size, blocks * vars_ + PAD, 128), f32), pltpu.VMEM((width, columns), f32),
            pltpu.SemaphoreType.DMA((4,)),
        ],
        compiler_params=params, name="final",
    )(smap, sarea, sums, back_map, base, last, *returned)
    final_state = final_state.reshape(size, blocks, vars_, 128).transpose(2, 0, 1, 3)
    final_state = final_state.reshape(vars_, size, columns)
    return (final_state, tracer_out)


def solution(mesh):
    in_specs = (
        P(None, None, ("member", "atm", "ocn")),
        P("atm", None, None, None),
        P(),
        P(),
        P(),
        P(("atm", "ocn")),
        P(("atm", "ocn"), None),
        P(("atm", "ocn")),
        P(("atm", "ocn")),
        P(None, "atm", ("member", "ocn")),
        P("atm", "ocn"),
        P(),
        P(),
        P(),
    )
    out_specs = (P(None, None, ("member", "atm", "ocn")), P(None, "atm", ("member", "ocn")))
    return jax.shard_map(
        on_device, mesh=mesh, in_specs=in_specs, out_specs=out_specs, check_vma=False
    )
```

```python
import functools
import jax
import jax.numpy as jnp
from jax import lax
from jax.experimental import pallas as pl
from jax.experimental.pallas import tpu as pltpu
from jax.sharding import PartitionSpec as P

OSTEPS = 4
PAD = 8
NVAR = 4
OY = 32
OX = 128
OCELLS = OY * OX
STRIPS = 8
f32 = jnp.float32
bf16 = jnp.bfloat16
i32 = jnp.int32


def nn(a, b):
    return jnp.dot(a, b, preferred_element_type=f32)


def nt(a, b):
    return lax.dot_general(a, b, (((1,), (1,)), ((), ())), preferred_element_type=f32)


def split(x):
    high = x.astype(bf16)
    return high, (x - high.astype(f32)).astype(bf16)


def three(dot, a, b):
    ah, al = split(a)
    bh, bl = split(b)
    return dot(ah, bh) + dot(ah, bl) + dot(al, bh)


def doubled(x):
    return jnp.concatenate(list(split(x)), axis=0)


def wide(left, right, dot=nn):
    count = left.shape[0] // 2
    high, low = split(right)
    both = dot(left, high)
    return both[:count] + both[count:] + dot(left[:count], low)


def column_block(ref, var, first, blocks):
    size, rows, lanes = ref.shape
    lines = ref.reshape(size * rows, lanes)
    step = NVAR
    return jnp.concatenate(
        [lines[pl.ds((first + i) * step + var, size, stride=rows), :] for i in range(blocks)],
        axis=1,
    )


def iota(shape, dim):
    return lax.broadcasted_iota(i32, shape, dim)


def flat(x):
    return jnp.concatenate([x[i : i + 1, :] for i in range(x.shape[0])], axis=1)


def onehot(row, size):
    return jnp.where(iota((size, row.shape[1]), 0) == row, 1.0, 0.0).astype(bf16)


def place(high, low, payloads, rows):
    lines = iota((rows, high.shape[1]), 0) == high
    left = jnp.concatenate([jnp.where(lines, p, 0.0) for p in payloads], axis=0).astype(bf16)
    out = nt(left, onehot(low, 128))
    return [out[i * rows : (i + 1) * rows] for i in range(len(payloads))]


def stacked(x):
    return jnp.concatenate([x[:, h : h + 256] for h in range(0, x.shape[1], 256)], axis=0)


def two_terms(ref):
    return jnp.concatenate([stacked(ref[0]), stacked(ref[1])], axis=1)


def gather(source, low, high, width, chunk=512):
    count = source.shape[0] // width
    outs = []
    for start in range(0, low.shape[1], chunk):
        stop = min(start + chunk, low.shape[1])
        hot = onehot(low[:, start:stop], 256)
        if source.shape[1] == 512:
            hot = jnp.concatenate([hot, hot], axis=0)
        part = nn(source, hot)
        hc = high[:, start:stop]
        total = jnp.where(hc == 0, part[:width], 0.0)
        for h in range(1, count):
            total = jnp.where(hc == h, part[h * width : (h + 1) * width], total)
        outs.append(total)
    return outs[0] if len(outs) == 1 else jnp.concatenate(outs, axis=1)


def spread(value, low, high, count):
    parts = [jnp.where(high == h, value, 0.0) for h in range(count)]
    return nt(jnp.concatenate(parts, axis=0).astype(bf16), onehot(low, 256))


def pick(level_rows, lane_rows, base):
    index = iota(level_rows.shape, 0)
    for i, row in enumerate(lane_rows):
        level_rows = jnp.where(index == base + i, row, level_rows)
    return level_rows


def roll(x, shift):
    shift = shift % 128
    return x if shift == 0 else pltpu.roll(x, shift, 1)


def row_of(x, y):
    return x[:, y * OX : (y + 1) * OX]


def border_block(x, lane):
    blocks = []
    for i in range(2):
        block = jnp.zeros((x.shape[0], OX), f32)
        for b in range(4):
            for j in range(4):
                first = b * 32 + j * 8
                moved = roll(row_of(x, b * 8 + i * 4 + j), first + 4)
                block = jnp.where((lane >= first) & (lane < first + 8), moved, block)
        blocks.append(block)
    return jnp.concatenate(blocks, axis=1)


def strips(x, halo, lane):
    outs = []
    for j in range(STRIPS):
        side = roll(row_of(halo, j // 4), 8 - (j % 4) * 8)
        for b in range(4):
            line = row_of(x, b * 8 + j)
            first = b * 32
            side = jnp.where((lane >= first) & (lane < first + 8), roll(line, first + 8), side)
            side = jnp.where(
                (lane >= first + 16) & (lane < first + 24), roll(line, first + 16), side
            )
        outs.append(side)
    return outs


def send_kernel(
    peers, levels, width, borders,
    *refs,
):
    sources, rest = refs[:11], refs[11:]
    packed_ref, rest = rest[0], rest[1:]
    side_refs, rest = rest[: len(borders)], rest[len(borders) :]
    (even_ref, odd_ref), rest = rest[:2], rest[2:]
    forcing_ref, t_ref, omap_ref, oarea_ref, smap_ref, sarea_ref, state_ref = rest[:7]
    staged, fw_pad, sems, state_sems = rest[7:17], rest[17], rest[18], rest[19]
    (area_ref, col_ref, dest_ref, cell_ref, class_ref, inv_ref, flux_ref, fw_ref, tracer_ref,
     land_ref) = staged
    loads = [
        pltpu.make_async_copy(a, b.at[:, pl.ds(0, OY), :] if b is tracer_ref else b, sems.at[i])
        for i, (a, b) in enumerate(zip(sources[:10], staged))
    ]
    for load in loads:
        load.start()
    state_hbm = sources[10]
    parts = state_sems.shape[0]
    part_rows = state_hbm.shape[1] // parts
    state_loads = []
    for i in range(parts):
        at = pl.ds(i * part_rows, part_rows)
        state_loads.append(
            pltpu.make_async_copy(
                state_hbm.at[:, at, :], state_ref.at[:, at, :], state_sems.at[i]
            )
        )
        state_loads[i].start()
    for load in loads[:5]:
        load.wait()
    me = lax.axis_index("ocn")
    slots = packed_ref.shape[1]
    slot_rows = slots // 128
    slot_pad = -(-slot_rows // 8) * 8
    lines = col_ref.shape[0]
    lane = iota((1, 128), 1)

    offset = (dest_ref[...] - me) & (peers - 1)
    cells = cell_ref[...]
    classes = class_ref[...]
    cols = col_ref[...]
    area = jnp.zeros(cols.shape, f32)
    for i in range(area_ref.shape[0]):
        area = jnp.where(classes == i, area_ref[i], area)

    hits = [jnp.where(offset == k, 1.0, 0.0) for k in range(1, peers)]
    hot = jnp.concatenate(hits, axis=0)
    upper = jnp.where(iota((128, 128), 0) <= iota((128, 128), 1), 1.0, 0.0).astype(bf16)
    running = nn(hot.astype(bf16), upper)
    count = running.shape[0]
    totals = jnp.broadcast_to(running[:, 127:128], running.shape).astype(bf16)
    below = jnp.where(iota((count, count), 1) < iota((count, count), 0), 1.0, 0.0).astype(bf16)
    before = nn(below, totals)
    place_of = running + before - 1.0
    slot = jnp.full(cols.shape, -1.0, f32)
    for k in range(1, peers):
        at = (k - 1) * lines
        slot = jnp.where(offset == k, place_of[at : at + lines], slot)
    slot = slot.astype(i32)
    position = iota((slot_pad, 128), 0) * 128 + iota((slot_pad, 128), 1)
    segment = jnp.full((slot_pad, 128), 1, i32)
    for k in range(2, peers):
        at = (k - 1) * lines
        start = before[at : at + 1, :].astype(i32)
        segment = segment + jnp.where(position >= start, 1, 0)

    a1 = area.astype(bf16).astype(f32)
    a2 = (area - a1).astype(bf16).astype(f32)
    a3 = area - a1 - a2
    slot_f, cell_f = flat(slot), flat(cells)
    col_f = flat(cols)
    areas = [flat(a1), flat(a2), flat(a3)]
    col_low = (col_f & 255).astype(f32)
    col_high = lax.shift_right_arithmetic(col_f, 8).astype(f32)
    cell_low = cell_f & 127
    cell_high = lax.shift_right_arithmetic(cell_f, 7)
    got = place(
        lax.shift_right_arithmetic(slot_f, 7), slot_f & 127,
        [col_low, col_high] + areas + [cell_high.astype(f32), cell_low.astype(f32)], slot_pad,
    )
    keep = [flat(g[:slot_rows]) for g in got]
    s_low, s_high = keep[0].astype(i32), keep[1].astype(i32)
    s_area = keep[2] + keep[3] + keep[4]
    smap_ref[0:1, :] = s_low
    smap_ref[1:2, :] = s_high
    smap_ref[2:3, :] = flat(segment[:slot_rows])
    sarea_ref[...] = s_area

    local_high = jnp.where(flat(offset) == 0, cell_high, -1)
    own = place(local_high, cell_low, [col_low, col_high + 1.0] + areas, OY)
    o_low, o_high = own[0].astype(i32), own[1].astype(i32) - 1
    o_area = own[2] + own[3] + own[4]
    omap_ref[0:1, :] = flat(o_low)
    omap_ref[1:2, :] = flat(o_high)
    oarea_ref[...] = flat(o_area)

    blank = jnp.zeros((2, 128), f32)
    edge = []
    for m in (own[0], own[1], o_area):
        block = blank
        for b in range(4):
            part = m[b * 8 : (b + 1) * 8]
            for j in range(4):
                first = b * 32 + j * 8
                moved = roll(part, first + 4)
                pair = jnp.concatenate([moved[j : j + 1], moved[4 + j : 5 + j]], axis=0)
                block = jnp.where((lane >= first) & (lane < first + 8), pair, block)
        edge.append(flat(block))

    for load in loads[5:]:
        load.wait()
    fw_pad[...] = jnp.zeros_like(fw_pad)
    fw_pad[0:levels, :] = fw_ref[...]
    fw = fw_pad[...]
    size = inv_ref.shape[0]
    flux = flux_ref[...].reshape(size * NVAR, flux_ref.shape[2])
    mixed = wide(doubled(fw), flux, nt)
    which = iota((1, size * NVAR), 1) & (NVAR - 1)
    masked = jnp.concatenate([jnp.where(which == v, mixed, 0.0) for v in range(NVAR)], axis=0)
    drawn = wide(doubled(masked), inv_ref[...].reshape(size * NVAR, size))
    pulled = [doubled(drawn[v * width : (v + 1) * width]) for v in range(NVAR)]

    tracer_lines = tracer_ref.reshape(levels * (OY + PAD), OX)
    for y in range(OY):
        at = pl.ds(y * OX, OX)
        t_ref[0:levels, at] = tracer_lines[pl.ds(y, levels, stride=OY + PAD), :]
        t_ref[levels : levels + 1, at] = land_ref[y : y + 1, :].astype(f32)
        t_ref[levels + 1 : width, at] = jnp.zeros((width - levels - 1, OX), f32)

    is_even = (lax.axis_index("atm") & 1) == 0
    top, bottom = t_ref[:, 0 : 4 * OX], t_ref[:, 28 * OX : 32 * OX]
    even_ref[...] = jnp.where(is_even, bottom, top).astype(bf16)
    odd_ref[...] = jnp.where(is_even, top, bottom).astype(bf16)

    for i in range(parts):
        state_loads[i].wait()
        for c in range(i * part_rows // NVAR, (i + 1) * part_rows // NVAR, 2):
            total = None
            for v in range(NVAR):
                term = wide(pulled[v], column_block(state_ref, v, c, 2))
                total = term if total is None else total + term
            at = slice(c * 128, (c + 2) * 128)
            forcing_ref[0, :, at], forcing_ref[1, :, at] = split(total)
    source = two_terms(forcing_ref)

    rows = gather(source, s_low, s_high, width) * s_area
    rows = pick(rows, keep[5:7], levels + 1).astype(bf16)
    packed_ref[...] = rows
    f_edge = gather(source, edge[0].astype(i32), edge[1].astype(i32) - 1, width) * edge[2]
    t_edge = border_block(t_ref[...], lane)
    lead = (lane & 7) < 4
    to_right, to_left = [], []
    for i in range(2):
        fe, te = row_of(f_edge, i), row_of(t_edge, i)
        to_right.append(jnp.where(lead, fe, roll(te, 4)))
        to_left.append(jnp.where(lead, roll(fe, -4), te))
    to_right = jnp.concatenate(to_right, axis=1)
    to_left = jnp.concatenate(to_left, axis=1)
    for mask, ref in zip(borders, side_refs):
        ref[:, 0:slots] = rows
        ref[:, slots : slots + 256] = jnp.where((me ^ mask) == me + 1, to_right, to_left).astype(
            bf16
        )


def local_kernel(width, forcing_ref, omap_ref, oarea_ref, out_ref):
    source = two_terms(forcing_ref)
    out_ref[...] = gather(source, omap_ref[0:1, :], omap_ref[1:2, :], width) * oarea_ref[...]


def receive_kernel(
    peers, levels, width, borders, early0, early1, packed_ref, smap_ref, local_ref, t_ref, *rest
):
    got = rest[: peers - 1]
    f_ref, fs_ref, ts_ref, cmap_ref, even_ref, odd_ref, edge_ref = rest[peers - 1 :]
    me = lax.axis_index("ocn")
    slots = packed_ref.shape[1]
    lane = iota((1, 128), 1)
    segment = smap_ref[2:3, :]
    chunks = slots // 256

    def meant_for(tile):
        total = jnp.zeros((width, slots), f32)
        for mask in range(peers):
            ref = packed_ref if mask == 0 else got[mask - 1]
            step = (tile - (me ^ mask)) & (peers - 1)
            total = jnp.where(segment == step, ref[:, 0:slots].astype(f32), total)
        high = total[levels + 1 : levels + 2, :].astype(i32)
        low = total[levels + 2 : levels + 3, :].astype(i32)
        return stacked(total.astype(bf16)), high, low

    index = iota((1, slots), 1)
    payload = [(index & 255).astype(f32), (lax.shift_right_arithmetic(index, 8) + 1).astype(f32)]

    source, high, low = meant_for(me)
    cell = high * 128 + low
    cmap_ref[0:1, :] = cell & 255
    cmap_ref[1:2, :] = lax.shift_right_arithmetic(cell, 8)
    where_low, where_high = place(high, low, payload, OY)
    f_ref[...] = local_ref[...] + gather(
        source, flat(where_low).astype(i32), flat(where_high).astype(i32) - 1, width
    )

    halo_f = None
    for step in (-1, 1):
        source, high, low = meant_for(me + step)
        at = low - 120 if step < 0 else low
        inside = (low >= 124) if step < 0 else (low < 4)
        block = lax.shift_right_arithmetic(high & 7, 2)
        spot = lax.shift_right_arithmetic(high, 3) * 32 + (high & 3) * 8 + at
        where_low, where_high = place(jnp.where(inside, block, -1), spot, payload, 8)
        part = gather(
            source, flat(where_low[:2]).astype(i32), flat(where_high[:2]).astype(i32) - 1, width
        )
        halo_f = part if halo_f is None else halo_f + part

    def side_from(tile):
        block = jnp.zeros((width, 256), f32)
        for mask in borders:
            block = jnp.where(
                (me ^ mask) == tile, got[mask - 1][:, slots : slots + 256].astype(f32), block
            )
        return block

    from_left, from_right = side_from(me - 1), side_from(me + 1)
    lead = (lane & 7) < 4
    side_f, side_t = [], []
    for i in range(2):
        fl, fr = row_of(from_left, i), row_of(from_right, i)
        side_f.append(jnp.where(lead, fr, roll(fl, 4)) + row_of(halo_f, i))
        side_t.append(jnp.where(lead, roll(fr, -4), fl))
    f_strips = strips(f_ref[...], jnp.concatenate(side_f, axis=1), lane)
    t_strips = strips(t_ref[...], jnp.concatenate(side_t, axis=1), lane)
    for j in range(STRIPS):
        fs_ref[:, j * OX : (j + 1) * OX] = f_strips[j]
        ts_ref[:, j * OX : (j + 1) * OX] = t_strips[j]

    def four(parts, first, source):
        block = jnp.zeros((width, OX), f32)
        for m in range(4):
            inside = (lane >= m * 32) & (lane < m * 32 + 32)
            block = jnp.where(inside, roll(parts[first + m], 32 * (m - source)), block)
        return block

    edges = [four(p, first, source) for p in (f_strips, t_strips)
             for first, source in ((0, 0), (4, 0), (0, 3), (4, 3))]
    edge_ref[...] = jnp.concatenate(edges, axis=1)
    top = jnp.concatenate([f_ref[:, 0 : 3 * OX], edges[0], edges[4]], axis=1)
    bottom = jnp.concatenate([f_ref[:, 29 * OX : 32 * OX], edges[3], edges[7]], axis=1)
    is_even = (lax.axis_index("atm") & 1) == 0
    even_ref[...] = jnp.where(is_even, bottom, top).astype(bf16)
    odd_ref[...] = jnp.where(is_even, top, bottom).astype(bf16)


def tile_row(ref, y):
    return ref[:, y * OX : (y + 1) * OX]


def not_there(lane):
    me, peers = lax.axis_index("ocn"), lax.axis_size("ocn")
    spot = lane & 31
    return ((me == 0) & (spot >= 12) & (spot < 16)) | (
        (me == peers - 1) & (spot >= 8) & (spot < 12)
    )


def fill_diffusivity(ref, dif_ref):
    width, levels = ref.shape[0], dif_ref.shape[1]
    diag = iota((width, levels), 0) == iota((width, levels), 1)
    column = jnp.sum(jnp.where(diag, dif_ref[...], 0.0), axis=1, keepdims=True)
    ref[...] = jnp.broadcast_to(column, ref.shape)


def count_rows(w8, n8, rows):
    for y in rows:
        here = tile_row(w8, y)
        n8[:, y * OX : (y + 1) * OX] = (
            tile_row(w8, y - 1) + tile_row(w8, y + 1) + roll(here, 1) + roll(here, -1)
        )


def substep_rows(rows, forcing, wet, counts, dif):
    for step in range(OSTEPS):
        new = list(rows)
        for y in range(step + 1, len(rows) - 1 - step):
            here = rows[y]
            lap = (rows[y - 1] + rows[y + 1] - counts(y) * here) + (roll(here, 1) + roll(here, -1))
            new[y] = here + wet(y) * (dif * lap + forcing(y))
        rows = new
    return rows


def substep_strips(now, forcing, wet, counts, dif, ends):
    for step in range(OSTEPS):
        new = []
        for j, here in enumerate(now):
            up, down = ends(now, j)
            lap = (roll(here, 1) + roll(here, -1) - counts[j] * here) + (up + down)
            new.append(here + wet[j] * (dif * lap + forcing[j]))
        now = new
    return now


def tall(ref, j, count):
    return jnp.concatenate([tile_row(ref, j)] * (count // 8), axis=0)


def merged(line, value, lane, b):
    value = jnp.where(lane < 4, roll(line, -(b * 32 + 16)), value)
    return jnp.where(lane >= 124, roll(line, 120 - b * 32), value)


def inner_kernel(
    levels, width, f_ref, fs_ref, t_ref, ts_ref, dif_ref, tt_ref, strip, w8, n8, ws8, ns8, d8
):
    lane = iota((1, 128), 1)
    w8[...] = jnp.broadcast_to(t_ref[levels : levels + 1, :], w8.shape)
    count_rows(w8, n8, range(1, OY - 1))
    outside = not_there(lane)
    for j in range(STRIPS):
        line = tile_row(ts_ref, j)[levels : levels + 1, :]
        ws8[:, j * OX : (j + 1) * OX] = jnp.broadcast_to(jnp.where(outside, 0.0, line), (8, OX))

    def ends(parts, j):
        up = roll(parts[STRIPS - 1], 32) if j == 0 else parts[j - 1]
        down = roll(parts[0], 96) if j == STRIPS - 1 else parts[j + 1]
        return up, down

    parts = [tile_row(ws8, j) for j in range(STRIPS)]
    for j in range(STRIPS):
        up, down = ends(parts, j)
        ns8[:, j * OX : (j + 1) * OX] = up + down + roll(parts[j], 1) + roll(parts[j], -1)
    fill_diffusivity(d8, dif_ref)

    lev = slice(0, width)

    def strip_group():

        def load(ref, j):
            return ref[lev, j * OX : (j + 1) * OX]

        wet = [tall(ws8, j, width) for j in range(STRIPS)]
        now = substep_strips(
            [load(ts_ref, j) * wet[j] for j in range(STRIPS)],
            [load(fs_ref, j) for j in range(STRIPS)], wet,
            [tall(ns8, j, width) for j in range(STRIPS)], d8[lev, :], ends,
        )
        for j in range(STRIPS):
            strip[lev, j * OX : (j + 1) * OX] = now[j]

    strip_group()

    def main():
        dif = d8[lev, :]

        def load(ref, j):
            return ref[lev, j * OX : (j + 1) * OX]

        rows = substep_rows(
            [load(t_ref, y) * tall(w8, y, width) for y in range(OY)], lambda y: load(f_ref, y),
            lambda y: tall(w8, y, width), lambda y: tall(n8, y, width), dif,
        )
        now = [load(strip, j) for j in range(STRIPS)]
        for y in range(4, OY - 4):
            value = merged(now[y % 8], rows[y], lane, y // 8)
            tt_ref[lev, y * OX : (y + 1) * OX] = jnp.where(
                tall(w8, y, width) > 0.0, value, load(t_ref, y)
            )

    main()


def slab_kernel(levels, t_ref, even_ref, odd_ref, s, w8, n8):
    row, rows_atm = lax.axis_index("atm"), lax.axis_size("atm")
    is_even = (row & 1) == 0
    even, odd = even_ref[...].astype(f32), odd_ref[...].astype(f32)
    top, bottom = jnp.where(is_even, odd, even), jnp.where(is_even, even, odd)
    tops = jnp.where(row > 0, 1.0, 0.0)
    bottoms = jnp.where(row < rows_atm - 1, 1.0, 0.0)

    def wide_wet(x):
        return jnp.broadcast_to(x[levels : levels + 1, :], (8, x.shape[1]))

    w8[:, 0 : 4 * OX] = wide_wet(top) * tops
    w8[:, 4 * OX : 12 * OX] = wide_wet(t_ref[:, 0 : 8 * OX])
    w8[:, 12 * OX : 20 * OX] = wide_wet(t_ref[:, 24 * OX : 32 * OX])
    w8[:, 20 * OX : 24 * OX] = wide_wet(bottom) * bottoms
    for y in (0, 11, 12, 23):
        n8[:, y * OX : (y + 1) * OX] = jnp.zeros((8, OX), f32)
    count_rows(w8, n8, list(range(1, 11)) + list(range(13, 23)))
    s[:, 0 : 4 * OX] = top * w8[0:1, 0 : 4 * OX]
    s[:, 4 * OX : 12 * OX] = t_ref[:, 0 : 8 * OX] * w8[0:1, 4 * OX : 12 * OX]
    s[:, 12 * OX : 20 * OX] = t_ref[:, 24 * OX : 32 * OX] * w8[0:1, 12 * OX : 20 * OX]
    s[:, 20 * OX : 24 * OX] = bottom * w8[0:1, 20 * OX : 24 * OX]


def outer_kernel(
    levels, width,
    f_ref, t_ref, edge_ref, inner_ref, even_ref, odd_ref, s, w8, n8, dif_ref, cmap_ref,
    tt_ref, back_ref,
    fx, se, we8, ne8, d8,
):
    row, rows_atm = lax.axis_index("atm"), lax.axis_size("atm")
    is_even = (row & 1) == 0
    lane = iota((1, 128), 1)
    block = lax.shift_right_arithmetic(lane, 5)
    even, odd = even_ref[...].astype(f32), odd_ref[...].astype(f32)
    top, bottom = jnp.where(is_even, odd, even), jnp.where(is_even, even, odd)
    tops = jnp.where(row > 0, 1.0, 0.0)
    bottoms = jnp.where(row < rows_atm - 1, 1.0, 0.0)

    def wide_wet(x):
        return jnp.broadcast_to(x[levels : levels + 1, :], (8, x.shape[1]))

    fx[:, OX : 4 * OX] = top[:, 0 : 3 * OX]
    fx[:, 4 * OX : 12 * OX] = f_ref[:, 0 : 8 * OX]
    fx[:, 12 * OX : 20 * OX] = f_ref[:, 24 * OX : 32 * OX]
    fx[:, 20 * OX : 23 * OX] = bottom[:, 0 : 3 * OX]
    outside = not_there(lane)
    for at, f_part, t_part, there in (
        (0, top[:, 384:512], top[:, 512:640], tops),
        (1, edge_ref[:, 0:128], edge_ref[:, 512:640], None),
        (2, edge_ref[:, 128:256], edge_ref[:, 640:768], None),
        (3, edge_ref[:, 256:384], edge_ref[:, 768:896], None),
        (4, edge_ref[:, 384:512], edge_ref[:, 896:1024], None),
        (5, bottom[:, 384:512], bottom[:, 512:640], bottoms),
    ):
        wet = jnp.where(outside, 0.0, wide_wet(t_part))
        wet = wet if there is None else wet * there
        we8[:, at * OX : (at + 1) * OX] = wet
        se[:, at * OX : (at + 1) * OX] = t_part * wet[0:1, :]
        se[:, (6 + at) * OX : (7 + at) * OX] = f_part

    def ends(parts, j):
        before = parts[j] if j % 3 == 0 else jnp.where(block == 3, parts[j - 1], parts[j])
        after = parts[j] if j % 3 == 2 else jnp.where(block == 0, parts[j + 1], parts[j])
        return roll(before, 32), roll(after, 96)

    parts = [tile_row(we8, j) for j in range(6)]
    for j in range(6):
        up, down = ends(parts, j)
        ne8[:, j * OX : (j + 1) * OX] = up + down + roll(parts[j], 1) + roll(parts[j], -1)
    fill_diffusivity(d8, dif_ref)
    tt_ref[:, 4 * OX : 28 * OX] = inner_ref[:, 4 * OX : 28 * OX]

    lev = slice(0, width)

    def strip_group():

        def load(ref, j):
            return ref[lev, j * OX : (j + 1) * OX]

        now = substep_strips(
            [load(se, j) for j in range(6)], [load(se, 6 + j) for j in range(6)],
            [tall(we8, j, width) for j in range(6)], [tall(ne8, j, width) for j in range(6)],
            d8[lev, :], ends,
        )
        se[lev, 0:OX], se[lev, OX : 2 * OX] = now[1], now[4]

    strip_group()

    def main():
        dif = d8[lev, :]

        def load(ref, j):
            return ref[lev, j * OX : (j + 1) * OX]

        slabs = []
        for base in (0, 12):
            slabs += substep_rows(
                [load(s, base + y) for y in range(12)], lambda y: load(fx, base + y),
                lambda y: tall(w8, base + y, width), lambda y: tall(n8, base + y, width), dif,
            )
        for m in range(4):
            for y, slab, line in ((m, 4 + m, load(se, 0)), (28 + m, 16 + m, load(se, 1))):
                value = merged(line, slabs[slab], lane, m)
                tt_ref[lev, y * OX : (y + 1) * OX] = jnp.where(
                    tall(w8, slab, width) > 0.0, value, load(t_ref, y)
                )

    main()
    source = stacked(tt_ref[...].astype(bf16))
    back_ref[...] = gather(source, cmap_ref[0:1, :], cmap_ref[1:2, :], width).astype(bf16)


def state_kernel(levels, inv_ref, sw_ref, sm_ref, state_ref, out_ref, h_ref, sm_pad, square):
    sm_pad[...] = jnp.zeros_like(sm_pad)
    sm_pad[0:levels, :] = sm_ref[...]
    h_ref[...] = jnp.zeros_like(h_ref)
    square[...] = jnp.zeros_like(square)
    blocks = (state_ref.shape[1] - PAD) // NVAR
    size = inv_ref.shape[0]
    room = h_ref.shape[0] // (2 * NVAR)
    for v in range(NVAR):
        inv = inv_ref[:, v, :]
        high, low = split(three(nn, inv, three(nt, sw_ref[:, v, :], sm_pad[...])))
        h_ref[v * room : v * room + size, :] = high
        h_ref[(NVAR + v) * room : (NVAR + v) * room + size, :] = low
        if v < NVAR - 1:
            square[v, 0:size, :], square[v, room : room + size, :] = split(three(nn, inv, inv))
    for v in range(NVAR - 1):
        for c in range(0, blocks, 2):
            value = wide(square[v], column_block(state_ref, v, c, 2))
            out_ref[v, :, c * 128 : (c + 2) * 128] = value[:size]


def late_state_kernel(after, inv_ref, state_ref, out_ref, square):
    square[...] = jnp.zeros_like(square)
    blocks = (state_ref.shape[1] - PAD) // NVAR
    size = inv_ref.shape[0]
    room = square.shape[0] // 2
    last = NVAR - 1
    inv = inv_ref[:, last, :]
    square[0:size, :], square[room : room + size, :] = split(three(nn, inv, inv))
    for c in range(0, blocks, 2):
        value = wide(square[...], column_block(state_ref, last, c, 2))
        out_ref[:, c * 128 : (c + 2) * 128] = value[:size]


def sum_kernel(levels, width, tt_ref, omap_ref, oarea_ref, out_ref, tracer_hbm, rows, sem):
    lines = rows.reshape(levels * (OY + PAD), OX)
    for y in range(OY):
        lines[pl.ds(y, levels, stride=OY + PAD), :] = tt_ref[0:levels, y * OX : (y + 1) * OX]
    store = pltpu.make_async_copy(rows.at[:, pl.ds(0, OY), :], tracer_hbm, sem)
    store.start()
    count = out_ref.shape[1] // 256
    chunk = 1024
    total = None
    for start in range(0, OCELLS, chunk):
        at = slice(start, start + chunk)
        value = tt_ref[:, at] * oarea_ref[:, at]
        value, rest = (term.astype(f32) for term in split(value))
        part = spread(value, omap_ref[0:1, at], omap_ref[1:2, at], count)
        part = part + spread(rest, omap_ref[0:1, at], omap_ref[1:2, at], count)
        total = part if total is None else total + part
    for h in range(count):
        out_ref[:, h * 256 : (h + 1) * 256] = total[h * width : (h + 1) * width]
    store.wait()


def final_kernel(
    peers, width, smap_ref, sarea_ref, sum_ref, h_ref, base_ref, last_ref, *rest
):
    got = rest[: peers - 1]
    out_hbm, rows, sums, sems = rest[peers - 1 :]
    columns = sum_ref.shape[1]
    count = columns // 256
    me = lax.axis_index("ocn")
    segment = smap_ref[2:3, :]
    total = jnp.zeros((width, segment.shape[1]), f32)
    for mask in range(1, peers):
        offset = ((me ^ mask) - me) & (peers - 1)
        total = jnp.where(segment == offset, got[mask - 1][...].astype(f32), total)
    part = spread(total * sarea_ref[...], smap_ref[0:1, :], smap_ref[1:2, :], count)
    for h in range(count):
        at = slice(h * 256, (h + 1) * 256)
        sums[:, at] = part[h * width : (h + 1) * width] + sum_ref[:, at]

    size, stride, lanes = rows.shape
    lines = rows.reshape(size * stride, lanes)
    parts = sems.shape[0]
    room = h_ref.shape[0] // (2 * NVAR)
    stores = []
    for i in range(parts):
        share = columns // parts
        for c in range(i * share, (i + 1) * share, 256):
            every = wide(h_ref[...], sums[:, c : c + 256])
            for v in range(NVAR):
                at = slice(c, c + 256)
                base = base_ref[v, :, at] if v < NVAR - 1 else last_ref[:, at]
                value = base + every[v * room : v * room + size]
                for k in range(2):
                    first = (c // 128 + k) * NVAR + v
                    lines[pl.ds(first, size, stride=stride), :] = value[:, k * 128 : k * 128 + 128]
        at = pl.ds(i * (share // 128 * NVAR), share // 128 * NVAR)
        store = pltpu.make_async_copy(rows.at[:, at, :], out_hbm.at[:, at, :], sems.at[i])
        store.start()
        stores.append(store)
    for store in stores:
        store.wait()


def on_device(
    atmos_state, inverses, flux_weight, surface_weight, area_table, xc_column, xc_dest, xc_cell,
    xc_class, tracer, land_sea, forcing_weight, surface_map, diffusivity,
):
    peers, tiles = lax.axis_size("ocn"), lax.axis_size("atm")
    vars_, size, columns = atmos_state.shape
    cells = xc_column.shape[0]
    levels = tracer.shape[0]
    slots = cells - 3 * cells // peers
    width = -(-(levels + 3) // 16) * 16
    borders = sorted({i ^ (i + 1) for i in range(peers - 1)})
    sds = jax.ShapeDtypeStruct
    params = pltpu.CompilerParams(vmem_limit_bytes=30 * 1024 * 1024)
    vmem = pl.BlockSpec(memory_space=pltpu.VMEM)

    def swap(x, axis, pairs):
        return lax.ppermute(x, axis, pairs)

    def xor_swap(x, mask):
        return swap(x, "ocn", [(i, i ^ mask) for i in range(peers)])

    blocks = columns // 128
    room = -(-size // 16) * 16
    by_level = lambda x: x.transpose(1, 0, 2)
    state = atmos_state.reshape(vars_, size, blocks, 128).transpose(1, 2, 0, 3)
    state = state.reshape(size, blocks * vars_, 128)
    inverse = by_level(inverses[0])
    hbm = pl.BlockSpec(memory_space=pltpu.HBM)
    anywhere = pl.BlockSpec(memory_space=pl.ANY)
    grid_of = lambda x: x.reshape(cells // 128, 128)
    small = [
        area_table, grid_of(xc_column), grid_of(xc_dest), grid_of(xc_cell), grid_of(xc_class),
        inverse, by_level(flux_weight), forcing_weight, tracer, land_sea,
    ]
    outs = pl.pallas_call(
        functools.partial(send_kernel, peers, levels, width, borders),
        out_shape=[sds((width, slots), bf16)]
        + [sds((width, slots + 256), bf16)] * len(borders)
        + [sds((width, 4 * OX), bf16)] * 2
        + [
            sds((2, width, columns), bf16), sds((width, OCELLS), f32), sds((2, OCELLS), i32),
            sds((1, OCELLS), f32), sds((3, slots), i32), sds((1, slots), f32),
            sds((size, blocks * vars_ + PAD, 128), f32),
        ],
        in_specs=[hbm] * 11,
        out_specs=[vmem] * (10 + len(borders)),
        scratch_shapes=[pltpu.SMEM(small[0].shape, f32)]
        + [pltpu.VMEM(x.shape, x.dtype) for x in small[1:8]]
        + [pltpu.VMEM((levels, OY + PAD, OX), f32), pltpu.VMEM(land_sea.shape, i32)]
        + [
            pltpu.VMEM((width, forcing_weight.shape[1]), f32),
            pltpu.SemaphoreType.DMA((len(small),)), pltpu.SemaphoreType.DMA((4,)),
        ],
        compiler_params=params,
        name="send",
    )(*[pltpu.with_memory_space_constraint(x, pltpu.HBM) for x in small + [state]])
    packed, sides = outs[0], outs[1 : 1 + len(borders)]
    even_t, odd_t, forcing_cols, t0, omap, oarea, smap, sarea, state = outs[1 + len(borders) :]
    got = []
    for mask in range(1, peers):
        buffer = sides[borders.index(mask)] if mask in borders else packed
        got.append(xor_swap(buffer, mask))

    first = [(i, i ^ 1) for i in range(tiles)]
    second = [(i, (i + 1) % tiles if i & 1 else (i - 1) % tiles) for i in range(tiles)]
    even_t, odd_t = swap(even_t, "atm", first), swap(odd_t, "atm", second)

    local = pl.pallas_call(
        functools.partial(local_kernel, width),
        out_shape=sds((width, OCELLS), f32),
        in_specs=[vmem] * 3, out_specs=vmem, compiler_params=params, name="local",
    )(forcing_cols, omap, oarea)

    slab = 24 * OX
    slabs = pl.pallas_call(
        functools.partial(slab_kernel, levels),
        out_shape=[sds((width, slab), f32), sds((8, slab), f32), sds((8, slab), f32)],
        in_specs=[vmem] * 3, out_specs=[vmem] * 3, compiler_params=params, name="slab",
    )(t0, even_t, odd_t)

    base, back_map = pl.pallas_call(
        functools.partial(state_kernel, levels),
        out_shape=[sds((vars_ - 1, size, columns), f32), sds((2 * vars_ * room, width), bf16)],
        in_specs=[vmem] * 4, out_specs=[vmem] * 2,
        scratch_shapes=[
            pltpu.VMEM((width, surface_map.shape[1]), f32),
            pltpu.VMEM((vars_ - 1, 2 * room, size), bf16),
        ],
        compiler_params=params, name="state",
    )(inverse, by_level(surface_weight), surface_map, state)

    send_rows = 5 * OX
    f_all, fs, ts, cmap, even, odd, edge = pl.pallas_call(
        functools.partial(receive_kernel, peers, levels, width, borders),
        out_shape=[
            sds((width, OCELLS), f32), sds((width, STRIPS * OX), f32),
            sds((width, STRIPS * OX), f32), sds((2, slots), i32),
            sds((width, send_rows), bf16), sds((width, send_rows), bf16),
            sds((width, 8 * OX), f32),
        ],
        in_specs=[anywhere] * 2 + [vmem] * (3 + peers), out_specs=[vmem] * 7,
        compiler_params=params, name="receive",
    )(slabs[2], back_map, packed, smap, local, t0, *got)
    even, odd = swap(even, "atm", first), swap(odd, "atm", second)

    dif = diffusivity.reshape(1, levels)
    scratch = lambda *shapes: [pltpu.VMEM(shape, f32) for shape in shapes]
    inner = pl.pallas_call(
        functools.partial(inner_kernel, levels, width),
        out_shape=sds((width, OCELLS), f32),
        in_specs=[vmem] * 5, out_specs=vmem,
        scratch_shapes=scratch(
            (width, STRIPS * OX), (8, OCELLS), (8, OCELLS), (8, STRIPS * OX), (8, STRIPS * OX),
            (width, OX),
        ),
        compiler_params=params, name="inner",
    )(f_all, fs, t0, ts, dif)
    t4, back = pl.pallas_call(
        functools.partial(outer_kernel, levels, width),
        out_shape=[sds((width, OCELLS), f32), sds((width, slots), bf16)],
        in_specs=[vmem] * 11, out_specs=[vmem] * 2,
        scratch_shapes=scratch(
            (width, slab), (width, 12 * OX), (8, 6 * OX), (8, 6 * OX), (width, OX),
        ),
        compiler_params=params, name="outer",
    )(f_all, t0, edge, inner, even, odd, *slabs, dif, cmap)

    returned = [xor_swap(back, mask) for mask in range(1, peers)]
    sums, tracer_out = pl.pallas_call(
        functools.partial(sum_kernel, levels, width),
        out_shape=[sds((width, columns), f32), pltpu.HBM(tracer.shape, f32)],
        in_specs=[vmem] * 3, out_specs=[vmem, hbm],
        scratch_shapes=[pltpu.VMEM((levels, OY + PAD, OX), f32), pltpu.SemaphoreType.DMA],
        compiler_params=params, name="sum",
    )(t4, omap, oarea)

    last = pl.pallas_call(
        late_state_kernel,
        out_shape=sds((size, columns), f32),
        in_specs=[anywhere] + [vmem] * 2, out_specs=vmem,
        scratch_shapes=[pltpu.VMEM((2 * room, size), bf16)],
        compiler_params=params, name="late_state",
    )(back, inverse, state)

    final_state = pl.pallas_call(
        functools.partial(final_kernel, peers, width),
        out_shape=pltpu.HBM((size, blocks * vars_, 128), f32),
        in_specs=[vmem] * (5 + peers), out_specs=hbm,
        scratch_shapes=[
            pltpu.VMEM((size, blocks * vars_ + PAD, 128), f32), pltpu.VMEM((width, columns), f32),
            pltpu.SemaphoreType.DMA((8,)),
        ],
        compiler_params=params, name="final",
    )(smap, sarea, sums, back_map, base, last, *returned)
    final_state = final_state.reshape(size, blocks, vars_, 128).transpose(2, 0, 1, 3)
    final_state = final_state.reshape(vars_, size, columns)
    return (final_state, tracer_out)


def solution(mesh):
    in_specs = (
        P(None, None, ("member", "atm", "ocn")),
        P("atm", None, None, None),
        P(),
        P(),
        P(),
        P(("atm", "ocn")),
        P(("atm", "ocn"), None),
        P(("atm", "ocn")),
        P(("atm", "ocn")),
        P(None, "atm", ("member", "ocn")),
        P("atm", "ocn"),
        P(),
        P(),
        P(),
    )
    out_specs = (P(None, None, ("member", "atm", "ocn")), P(None, "atm", ("member", "ocn")))
    return jax.shard_map(
        on_device, mesh=mesh, in_specs=in_specs, out_specs=out_specs, check_vma=False
    )
```
